128 devices in a mesh: frame: 16 (over y, x), head: 8 (over z, core).
Axes of the slice: x: 4, y: 4, z: 4, core: 2. Of those that a mesh axis runs over, the one named last changes fastest.
Arguments:
- tokens: bfloat16 [12288, 5120], P('frame', 'head'), may hold values from -40 to 40
- mask_block_frame: int32 [96], replicated, may hold values from 0 to 7, as said below
- attended_key_blocks: int32 [96, 10], replicated, may hold values from 0 to 95, as said below
- frozen_query_key_value: bfloat16 [5120, 3, 3072], P(None, None, 'head'), may hold values from -0.104815686 to 0.104815686
- query_key_value_down_weight: bfloat16 [5120, 192], replicated, may hold values from -0.078125 to 0.078125
- query_key_value_up_weight: bfloat16 [64, 3, 3072], P(None, None, 'head'), may hold values from -0.375 to 0.375
- frozen_output_weight: bfloat16 [3072, 5120], P('head'), may hold values from -0.109375 to 0.109375
- output_down_weight: bfloat16 [3072, 64], P('head'), may hold values from -0.109375 to 0.109375
- output_up_weight: bfloat16 [64, 5120], P(None, 'head'), may hold values from -0.75 to 0.75
Outputs:
- attended_out: bfloat16 [12288, 5120], P('frame', 'head')
The draws below stay inside these ranges and needn't reach their ends.
Inputs may be any that keep to these rules, and one draw needn't show every extreme that they name: `mask_block_frame`: Non-decreasing along the blocks; every frame from 0 to 7 holds at least one block. `attended_key_blocks`: row b lists 10 distinct key blocks and always includes b itself. Take aligned groups of 6 blocks; for a group of query blocks and another group g groups away (g >= 1), the rows of the first group together name exactly 4 // 2 ** (g - 1) distinct blocks of the second, except that a group exactly 8 groups away is named by exactly the larger of that number and 2.
All inputs are finite; a program needn't handle non-finite values.
Results may differ from the reference program's by a relative error of at most 0.017.
Values may be sent and summed in bfloat16 or wider, within the bound.
A program may use at most 128 MiB of HBM per device.

```python
import math
import jax
import jax.numpy as jnp
from jax import lax

MODEL_WIDTH = 5120
ATTENTION_HEADS = 24
HEAD_SIZE = 128
ADAPTER_RANK = 64
BLOCK = 128
LISTED = 10
PEER_BLOCKS = 4
CLIP_TOKENS = 12288
BLOCKS_DEV = 6
NBLOCKS = 96
FRAMES = 8
N_HEAD = 8


def frame_of_blocks(key):
    cut_key = jax.random.fold_in(key, 11)
    shuffled = jax.random.permutation(cut_key, NBLOCKS - 1) + 1
    cut_points = jnp.sort(shuffled[:FRAMES - 1])
    all_blocks = jnp.arange(NBLOCKS, dtype=jnp.int32)
    return jnp.sum((all_blocks[:, None] >= cut_points[None, :]).astype(jnp.int32), axis=1).astype(jnp.int32)


def draw_mask_block_frame(key, part):
    return frame_of_blocks(key)


def draw_attended_key_blocks(key, part):
    frame_ids = frame_of_blocks(key)
    all_blocks = jnp.arange(NBLOCKS, dtype=jnp.int32)
    same_frame = frame_ids[:, None] == frame_ids[None, :]
    first_block = jnp.min(jnp.where(same_frame, all_blocks[None, :], NBLOCKS), axis=1)
    place = all_blocks - first_block
    groups = NBLOCKS // BLOCKS_DEV
    owner_dev = all_blocks // BLOCKS_DEV
    within = all_blocks % BLOCKS_DEV
    rank_key = jax.random.fold_in(key, 23)
    raw_score = jax.random.randint(rank_key, (groups, groups, BLOCKS_DEV), 0, 4096) * BLOCKS_DEV + jnp.arange(BLOCKS_DEV, dtype=jnp.int32)[None, None, :]
    ordering = jnp.argsort(raw_score, axis=2, stable=True)
    block_rank = jnp.argsort(ordering, axis=2, stable=True).astype(jnp.int32)
    group_ids = jnp.arange(groups, dtype=jnp.int32)
    distance = jnp.abs(group_ids[:, None] - group_ids[None, :])
    near_quota = jnp.where(distance >= 1, PEER_BLOCKS // 2 ** jnp.clip(distance - 1, 0, 20), 0).astype(jnp.int32)
    quota = jnp.where(distance == groups // 2, jnp.maximum(near_quota, PEER_BLOCKS // 2), near_quota).astype(jnp.int32)
    visible = block_rank < quota[:, :, None]
    peer_slot = group_ids[None, :] - (group_ids[None, :] > group_ids[:, None]).astype(jnp.int32)
    order_number = peer_slot[:, :, None] * PEER_BLOCKS + block_rank
    query_owner = owner_dev[:, None]
    key_owner = owner_dev[None, :]
    key_within = within[None, :]
    seen = visible[query_owner, key_owner, key_within]
    needed = seen & (order_number[query_owner, key_owner, key_within] % BLOCKS_DEV == within[:, None])
    allowed = (query_owner == key_owner) | seen
    itself = all_blocks[:, None] == all_blocks[None, :]
    tier = jnp.where(needed | itself, 0, jnp.where(allowed, 1, 2)).astype(jnp.int32)
    frame_gap = jnp.minimum(jnp.abs(frame_ids[:, None] - frame_ids[None, :]), 10)
    spread = (jnp.abs(place[:, None] - place[None, :]) + 1) * 2 ** frame_gap
    jitter = jax.random.randint(jax.random.fold_in(key, 31), (NBLOCKS, NBLOCKS), 0, 4)
    spread = jnp.minimum(spread, 2 ** 14) * 4 + jitter
    score = tier * 2 ** 27 + spread * NBLOCKS + all_blocks[None, :]
    unused, picked = lax.top_k(-score, LISTED)
    return picked.astype(jnp.int32)


def draw_tokens(key, part):
    first_key = jax.random.fold_in(key, 0)
    normal_part = jnp.clip(jax.random.normal(first_key, (CLIP_TOKENS, MODEL_WIDTH), jnp.float32), -6.0, 6.0)
    return normal_part.astype(jnp.bfloat16)


def draw_frozen_query_key_value(key, part):
    first_key = jax.random.fold_in(key, 0)
    shape_full = (MODEL_WIDTH, 3, ATTENTION_HEADS * HEAD_SIZE)
    weights = jnp.clip(jax.random.normal(first_key, shape_full, jnp.float32), -6.0, 6.0) / math.sqrt(MODEL_WIDTH)
    return weights.astype(jnp.bfloat16)


def level_of(stream_key, shape, cuts, low, top_value):
    loudness, own = 1.0, jax.random.fold_in(stream_key, 6)
    for position, blocks in cuts:
        draws = jnp.exp(jax.random.uniform(jax.random.fold_in(own, position), (blocks,), jnp.float32, low / len(cuts), top_value / len(cuts)))
        loudness = loudness * jnp.repeat(draws, shape[position] // blocks).reshape([-1 if axis == position else 1 for axis in range(len(shape))])
    return loudness


def noise(key, shape, deviation, most, cuts=(), kind=jnp.bfloat16):
    entries = deviation * jax.random.normal(key, shape, jnp.float32)
    if cuts:
        entries = entries * level_of(key, shape, cuts, -0.22, 0.18)
    return jnp.clip(entries, -most, most).astype(kind)


def setup_inputs(seed: int = 0) -> dict:
    streams_of = jax.random.split(jax.random.key(seed), 10)
    return {
        "tokens": draw_tokens(jax.random.fold_in(streams_of[9], 71), 0),
        "mask_block_frame": draw_mask_block_frame(jax.random.fold_in(streams_of[9], 71), 0),
        "attended_key_blocks": draw_attended_key_blocks(jax.random.fold_in(streams_of[9], 71), 0),
        "frozen_query_key_value": draw_frozen_query_key_value(jax.random.fold_in(streams_of[9], 71), 0),
        "query_key_value_down_weight": noise(streams_of[4], (MODEL_WIDTH, 3 * ADAPTER_RANK), MODEL_WIDTH ** -0.5, 0.078125),
        "query_key_value_up_weight": noise(streams_of[5], (ADAPTER_RANK, 3, ATTENTION_HEADS * HEAD_SIZE), (4 * ADAPTER_RANK) ** -0.5, 0.375, ((2, 8),)),
        "frozen_output_weight": noise(streams_of[6], (ATTENTION_HEADS * HEAD_SIZE, MODEL_WIDTH), (ATTENTION_HEADS * HEAD_SIZE) ** -0.5, 0.109375, ((0, 8),)),
        "output_down_weight": noise(streams_of[7], (ATTENTION_HEADS * HEAD_SIZE, ADAPTER_RANK), (ATTENTION_HEADS * HEAD_SIZE) ** -0.5, 0.109375, ((0, 8),)),
        "output_up_weight": noise(streams_of[8], (ADAPTER_RANK, MODEL_WIDTH), ADAPTER_RANK ** -0.5, 0.75, ((1, 8),)),
    }


def rotate_pairs(values, frame_pos, place):
    time_pairs = (HEAD_SIZE - 4 * (HEAD_SIZE // 6)) // 2
    space_pairs = (HEAD_SIZE - 2 * time_pairs) // 2
    time_freq = 10000.0 ** (-jnp.arange(time_pairs).astype(jnp.float32) / time_pairs)
    space_freq = 10000.0 ** (-jnp.arange(space_pairs).astype(jnp.float32) / space_pairs)
    time_angle = frame_pos[:, None] * time_freq[None, :]
    space_angle = place[:, None] * space_freq[None, :]
    cos_time = jnp.cos(time_angle)[:, None, :]
    sin_time = jnp.sin(time_angle)[:, None, :]
    cos_space = jnp.cos(space_angle)[:, None, :]
    sin_space = jnp.sin(space_angle)[:, None, :]
    first_part = values[:, :, :time_pairs]
    second_part = values[:, :, time_pairs:2 * time_pairs]
    third_part = values[:, :, 2 * time_pairs:2 * time_pairs + space_pairs]
    fourth_part = values[:, :, 2 * time_pairs + space_pairs:]
    return jnp.concatenate([first_part * cos_time - second_part * sin_time, first_part * sin_time + second_part * cos_time, third_part * cos_space - fourth_part * sin_space, third_part * sin_space + fourth_part * cos_space], axis=-1)

def token_positions(mask_block_frame, block_ids):
    count_blocks = mask_block_frame.shape[0]
    all_blocks = jnp.arange(count_blocks).astype(jnp.int32)
    same_frame = mask_block_frame[:, None] == mask_block_frame[None, :]
    first_block = lax.optimization_barrier(jnp.min(jnp.where(same_frame, all_blocks[None, :], count_blocks), axis=1)).astype(jnp.int32)
    inner_ids = jnp.arange(BLOCK).astype(jnp.int32)
    token_ids = block_ids[:, None] * BLOCK + inner_ids[None, :]
    frame_pos = jnp.broadcast_to(mask_block_frame[block_ids][:, None], token_ids.shape).reshape(-1).astype(jnp.float32)
    place = (token_ids - first_block[block_ids][:, None] * BLOCK).reshape(-1).astype(jnp.float32)
    return (frame_pos, place)

def reference(tokens, mask_block_frame, attended_key_blocks, frozen_query_key_value, query_key_value_down_weight, query_key_value_up_weight, frozen_output_weight, output_down_weight, output_up_weight):
    width = ATTENTION_HEADS * HEAD_SIZE
    adapter_query_key_value = jnp.dot(tokens, query_key_value_down_weight, preferred_element_type=jnp.float32).astype(jnp.bfloat16)
    adapter_query_key_value = lax.optimization_barrier(adapter_query_key_value)
    projected_rows = jnp.dot(tokens, frozen_query_key_value.reshape(MODEL_WIDTH, 3 * width), preferred_element_type=jnp.float32).reshape(CLIP_TOKENS, 3, width)
    projected_rows = projected_rows + jnp.einsum('ngc,cgz->ngz', adapter_query_key_value.reshape(CLIP_TOKENS, 3, ADAPTER_RANK).astype(jnp.float32), query_key_value_up_weight.astype(jnp.float32))
    frame_pos, place = token_positions(mask_block_frame, jnp.arange(NBLOCKS).astype(jnp.int32))
    queries = rotate_pairs(projected_rows[:, 0].reshape(CLIP_TOKENS, ATTENTION_HEADS, HEAD_SIZE), frame_pos, place).astype(jnp.bfloat16)
    keys = rotate_pairs(projected_rows[:, 1].reshape(CLIP_TOKENS, ATTENTION_HEADS, HEAD_SIZE), frame_pos, place).astype(jnp.bfloat16)
    values = projected_rows[:, 2].reshape(CLIP_TOKENS, ATTENTION_HEADS, HEAD_SIZE).astype(jnp.bfloat16)
    query_tiles = queries.reshape(NBLOCKS, BLOCK, ATTENTION_HEADS, HEAD_SIZE)
    key_tiles = keys.reshape(NBLOCKS, BLOCK, ATTENTION_HEADS, HEAD_SIZE)
    value_tiles = values.reshape(NBLOCKS, BLOCK, ATTENTION_HEADS, HEAD_SIZE)

    def attend_block(inputs):
        query_tile, chosen = inputs
        key_rows = key_tiles[chosen].reshape(LISTED * BLOCK, ATTENTION_HEADS, HEAD_SIZE).astype(jnp.float32)
        value_rows = value_tiles[chosen].reshape(LISTED * BLOCK, ATTENTION_HEADS, HEAD_SIZE).astype(jnp.float32)
        scores = jnp.einsum('qhd,khd->hqk', query_tile.astype(jnp.float32), key_rows) / math.sqrt(HEAD_SIZE)
        row_max = lax.optimization_barrier(jnp.max(scores, axis=-1, keepdims=True))
        powers = jnp.exp(scores - row_max)
        probs = (powers / lax.optimization_barrier(jnp.sum(powers, axis=-1, keepdims=True))).astype(jnp.bfloat16)
        probs = lax.optimization_barrier(probs)
        return jnp.einsum('hqk,khd->qhd', probs.astype(jnp.float32), value_rows).astype(jnp.bfloat16)
    attention_result = lax.map(attend_block, (query_tiles, attended_key_blocks)).reshape(CLIP_TOKENS, width)
    adapter_output = jnp.dot(attention_result, output_down_weight, preferred_element_type=jnp.float32).astype(jnp.bfloat16)
    group_width = width // N_HEAD

    def add_group(totals, group):
        columns = lax.dynamic_slice_in_dim(attention_result, group * group_width, group_width, 1)
        weight_rows = lax.dynamic_slice_in_dim(frozen_output_weight, group * group_width, group_width, 0)
        partial_value = jnp.dot(columns, weight_rows, preferred_element_type=jnp.float32).astype(jnp.bfloat16)
        partial_value = lax.optimization_barrier(partial_value)
        return (totals + partial_value.astype(jnp.float32), None)
    frozen_output, unused = lax.scan(add_group, jnp.zeros((CLIP_TOKENS, MODEL_WIDTH), jnp.float32), jnp.arange(N_HEAD).astype(jnp.int32))
    return (frozen_output + jnp.dot(adapter_output, output_up_weight, preferred_element_type=jnp.float32)).astype(jnp.bfloat16)
```

```python
import functools
import math

import jax
import jax.numpy as jnp
import numpy as np
from jax import lax
from jax.experimental import pallas as pl
from jax.experimental.pallas import tpu as pltpu
from jax.sharding import PartitionSpec as P

MODEL_WIDTH = 5120
HEAD_SIZE = 128
BLOCK = 128
LISTED = 10
NBLK = 6
GROUPS = 16
NB = 96
RANK = 64
HEADS = 3
SHARD = 640
TIME_PAIRS = 22
SPACE_PAIRS = 42
MESH = pl.DeviceIdType.MESH
F32 = jnp.float32
BF16 = jnp.bfloat16

OFFSETS = ((1, 0, 4), (-1, 4, 4), (2, 8, 2), (-2, 10, 2), (3, 12, 1), (-3, 13, 1), (8, 14, 2))
SLOTS = 16


def rope_constants():
    lanes = np.zeros((8, 128), np.float64)
    t = 10000.0 ** (-np.arange(TIME_PAIRS) / TIME_PAIRS)
    s = 10000.0 ** (-np.arange(SPACE_PAIRS) / SPACE_PAIRS)
    lanes[0] = np.concatenate([t, t, s, s])
    lanes[1] = np.concatenate(
        [-np.ones(TIME_PAIRS), np.ones(TIME_PAIRS), -np.ones(SPACE_PAIRS), np.ones(SPACE_PAIRS)]
    )
    lanes[2, : 2 * TIME_PAIRS] = 1.0
    return lanes.astype(np.float32)


def sin_cos(x):
    turns = jnp.floor(x * (1.0 / (2.0 * math.pi)) + 0.5)
    c1 = 6.28125
    c2 = float(np.float32(np.round((2 * math.pi - c1) * 2**20) / 2**20))
    c3 = 2 * math.pi - c1 - c2
    r = ((x - turns * c1) - turns * c2) - turns * c3
    r2 = r * r
    s = jnp.full_like(r, -1.0 / math.factorial(19))
    for n in (17, 15, 13, 11, 9, 7, 5, 3, 1):
        s = s * r2 + (1.0 if n % 4 == 1 else -1.0) / math.factorial(n)
    c = jnp.full_like(r, 1.0 / math.factorial(20))
    for n in (18, 16, 14, 12, 10, 8, 6, 4, 2, 0):
        c = c * r2 + (1.0 if n % 4 == 0 else -1.0) / math.factorial(n)
    return s * r, c


def kernel(
    tok, tabv, tabs, mbf, consts, wq, dn, up,
    out,
    xg, wv, dnv, upv, cosv, sinv, planv, plans, acc, accl, qv, own, sb, pool0, pool1, pool2, sc,
    loc_sem, ag_send, ag_recv, kv_send, kv_recv, plan_sem,
):
    f = lax.axis_index("frame")
    h = lax.axis_index("head")
    z = h // 2
    core = h % 2
    up_h = ((z + 1) % 4) * 2 + core
    dn_h = ((z + 3) % 4) * 2 + core
    far_h = ((z + 2) % 4) * 2 + core
    other = z * 2 + (1 - core)
    f8 = (f + 8) % GROUPS
    pools = (pool0, pool1, pool2)

    def target(d):
        if d == 8:
            return f8, None
        dst = f + d
        return dst, (dst >= 0) & (dst < GROUPS)

    rows_all = pl.ds(0, NBLK * BLOCK)
    ld_tok = pltpu.make_async_copy(
        tok, xg.at[rows_all, pl.ds(pl.multiple_of(h * SHARD, 128), SHARD)], loc_sem.at[0]
    )
    ld_w = pltpu.make_async_copy(wq, wv, loc_sem.at[1])
    ld_dn = pltpu.make_async_copy(dn, dnv, loc_sem.at[2])
    ld_tok.start()
    ld_w.start()
    ld_dn.start()

    barrier = pltpu.get_barrier_semaphore()
    for hh in (up_h, dn_h, other):
        pl.semaphore_signal(barrier, inc=1, device_id=(f, hh), device_id_type=MESH)
    for d, _, _ in OFFSETS:
        dst, ok = target(d)

        def greet(dst=dst):
            pl.semaphore_signal(barrier, inc=1, device_id=(dst, h), device_id_type=MESH)

        if ok is None:
            greet()
        else:
            pl.when(ok)(greet)
    count = 4
    for d in (1, -1, 2, -2, 3, -3):
        count = count + ((f + d >= 0) & (f + d < GROUPS)).astype(jnp.int32)
    pl.semaphore_wait(barrier, count)

    def cols(hh):
        return pl.ds(pl.multiple_of(hh * SHARD, 128), SHARD)

    def rows(r, start=0, size=BLOCK):
        return pl.ds(pl.multiple_of(r * BLOCK + start, 64), size)

    def ag_copy(kind, r, src_h, dst_h, start=0, size=BLOCK, from_tok=False):
        dst = xg.at[rows(r, start, size), cols(src_h)]
        src = tok.at[rows(r, start, size), :] if from_tok else dst
        return pltpu.make_async_remote_copy(
            src_ref=src, dst_ref=dst, send_sem=ag_send.at[kind, r], recv_sem=ag_recv.at[kind, r],
            device_id=(f, dst_h), device_id_type=MESH,
        )

    HALF = BLOCK // 2
    def own_up(r):
        return ag_copy(0, r, h, up_h, from_tok=True)

    def own_dn(r):
        return ag_copy(1, r, h, dn_h, from_tok=True)

    def own_other(r):
        return ag_copy(2, r, h, other, from_tok=True)

    def relay_up(r):
        return ag_copy(3, r, dn_h, up_h, 0, HALF)

    def relay_dn(r):
        return ag_copy(4, r, up_h, dn_h, HALF, HALF)

    def share_dn(r):
        return ag_copy(5, r, dn_h, other)

    def share_up(r):
        return ag_copy(6, r, up_h, other)

    def share_far0(r):
        return ag_copy(7, r, far_h, other, 0, HALF)

    def share_far1(r):
        return ag_copy(8, r, far_h, other, HALF, HALF)

    def start_own(r):
        own_up(r).start()
        own_dn(r).start()
        own_other(r).start()

    start_own(0)
    start_own(1)

    tab = tabv[...]
    gi = lax.broadcasted_iota(jnp.int32, (NB, NB), 0)
    ri = lax.broadcasted_iota(jnp.int32, (NB, NB), 1)
    member = jnp.zeros((NB, NB), F32)
    for k in range(LISTED):
        member = jnp.maximum(member, (jnp.broadcast_to(tab[k : k + 1, :], (NB, NB)) == gi).astype(F32))
    rq = lax.broadcasted_iota(jnp.int32, (NB, 128), 0)
    qq = lax.broadcasted_iota(jnp.int32, (NB, 128), 1)
    in_group = ((rq * 43) >> 8 == qq).astype(F32)
    used = (jnp.dot(member, in_group, preferred_element_type=F32) > 0.5).astype(F32)
    lower = (((gi * 43) >> 8 == (ri * 43) >> 8) & (ri < gi)).astype(F32)
    rank = jnp.dot(lower, used, preferred_element_type=F32)
    code = jnp.where(used > 0.5, rank, -1.0)
    mine = jnp.sum(jnp.where(qq == f, rank, 0.0), axis=1, keepdims=True)
    delta = ((rq * 43) >> 8) - f
    base = jnp.zeros((NB, 128), F32)
    for d, slot, _ in OFFSETS:
        hit = (delta == -d) if d != 8 else ((delta == 8) | (delta == -8))
        base = jnp.where(hit, float(NBLK + slot), base)
    place = jnp.where(delta == 0, (rq - NBLK * f).astype(F32), base + mine)
    planv[...] = jnp.where(qq == 127, place, code).astype(jnp.int32)
    plan_cp = pltpu.make_async_copy(planv, plans, plan_sem)
    plan_cp.start()

    freq = consts[0:1, :]
    sign = consts[1:2, :]
    timed = consts[2:3, :] > 0.5
    inner = lax.broadcasted_iota(jnp.int32, (BLOCK, 128), 0)

    def table(b, carry):
        g = f * NBLK + b
        fr = mbf[g]

        def tally(i, n):
            return n + (mbf[i] < fr).astype(jnp.int32)

        first = lax.fori_loop(0, NB, tally, jnp.int32(0))
        pos = ((g - first) * BLOCK + inner).astype(F32)
        frame_pos = jnp.zeros((BLOCK, 128), F32) + fr.astype(F32)
        angle = jnp.where(jnp.broadcast_to(timed, (BLOCK, 128)), frame_pos, pos) * freq
        sn, cs = sin_cos(angle)
        cosv[rows(b), :] = cs
        sinv[rows(b), :] = sn * sign
        return carry

    lax.fori_loop(0, NBLK, table, 0)

    upv[...] = jnp.zeros_like(upv)
    for s in range(3):
        upv[s, s * RANK : (s + 1) * RANK, :] = up[s]

    ld_tok.wait()
    ld_w.wait()
    ld_dn.wait()
    plan_cp.wait()

    lane = lax.broadcasted_iota(jnp.int32, (BLOCK, 128), 1)

    def rope(u, cs, sn):
        rot = jnp.where(
            lane < TIME_PAIRS,
            pltpu.roll(u, 128 - TIME_PAIRS, 1),
            jnp.where(
                lane < 2 * TIME_PAIRS,
                pltpu.roll(u, TIME_PAIRS, 1),
                jnp.where(
                    lane < 2 * TIME_PAIRS + SPACE_PAIRS,
                    pltpu.roll(u, 128 - SPACE_PAIRS, 1),
                    pltpu.roll(u, SPACE_PAIRS, 1),
                ),
            ),
        )
        return u * cs + rot * sn

    KC = 1280

    def compute(r):
        def step(k, carry):
            ks = pl.ds(pl.multiple_of(k * KC, 128), KC)
            xk = xg[rows(r), ks]
            keep = (k > 0).astype(F32)
            for s in range(3):
                part = jnp.dot(xk, wv[s, ks, :], preferred_element_type=F32)
                acc[s] = jnp.where(k > 0, acc[s], 0.0) + part
            low = lax.dot_general(xk, dnv[:, ks], (((1,), (1,)), ((), ())), preferred_element_type=F32)
            accl[...] = jnp.where(k > 0, accl[...], 0.0) + low
            return carry

        lax.fori_loop(0, MODEL_WIDTH // KC, step, 0)
        low = accl[...].astype(BF16)
        cs = cosv[rows(r), :]
        sn = sinv[rows(r), :]
        for s in range(3):
            y = acc[s] + jnp.dot(low, upv[s], preferred_element_type=F32)
            for a in range(HEADS):
                u = y[:, a * 128 : (a + 1) * 128]
                if s == 0:
                    qv[a, rows(r), :] = rope(u, cs, sn).astype(BF16)
                elif s == 1:
                    k = rope(u, cs, sn).astype(BF16)
                    own[a, r, 0] = k
                    pools[a][r, 0] = k
                else:
                    v = u.astype(BF16)
                    own[a, r, 1] = v
                    pools[a][r, 1] = v

    def kv_copy(a, slot, dst):
        return pltpu.make_async_remote_copy(
            src_ref=sb.at[a, slot], dst_ref=pools[a].at[NBLK + slot],
            send_sem=kv_send.at[a, slot], recv_sem=kv_recv.at[a, slot],
            device_id=(dst, h), device_id_type=MESH,
        )

    def send_slot(d, slot, rank_of):
        dst, ok = target(d)

        def go():
            idx = jnp.int32(0)
            for b in range(1, NBLK):
                idx = jnp.where(plans[f * NBLK + b, dst] == rank_of, b, idx)
            for a in range(HEADS):
                sb[a, slot] = own[a, idx]
                kv_copy(a, slot, dst).start()

        if ok is None:
            go()
        else:
            pl.when(ok)(go)

    def finish(r):
        relay_up(r).wait_recv()
        share_far0(r).start()
        relay_dn(r).wait_recv()
        share_far1(r).start()
        own_other(r).wait_recv()
        share_dn(r).wait_recv()
        share_up(r).wait_recv()
        share_far0(r).wait_recv()
        share_far1(r).wait_recv()
        compute(r)
        for ready in range(NBLK):
            slots = [
                (d, first + i, i)
                for d, first, n in OFFSETS
                for i in range(n)
                if NBLK - n + i == ready
            ]
            if slots:

                @pl.when(r == ready)
                def _():
                    for d, slot, i in slots:
                        send_slot(d, slot, i)

    def ring(r, carry):
        own_up(r).wait_recv()
        relay_up(r).start()
        share_dn(r).start()
        own_dn(r).wait_recv()
        relay_dn(r).start()
        share_up(r).start()

        @pl.when(r + 2 < NBLK)
        def _():
            start_own(r + 2)

        @pl.when(r > 0)
        def _():
            finish(r - 1)

        return carry

    lax.fori_loop(0, NBLK, ring, 0)
    finish(NBLK - 1)

    def drain(r, carry):
        for cp in (own_up, own_dn, own_other, relay_up, relay_dn, share_dn, share_up, share_far0, share_far1):
            cp(r).wait_send()
        return carry

    scale = math.log2(math.e) / math.sqrt(HEAD_SIZE)

    def attend(a, b, carry):
        pool = pools[a]
        q = qv[a, rows(b), :]
        idx = [
            jnp.clip(plans[tabs[k, f * NBLK + b], 127], 0, NBLK + SLOTS - 1) for k in range(LISTED)
        ]
        top = None
        for k in range(0, LISTED, 2):
            kk = jnp.concatenate([pool[idx[k], 0], pool[idx[k + 1], 0]], axis=0)
            s = lax.dot_general(q, kk, (((1,), (1,)), ((), ())), preferred_element_type=F32)
            sc[:, k * 128 : (k + 2) * 128] = s
            part = jnp.maximum(s[:, :128], s[:, 128:])
            top = part if top is None else jnp.maximum(top, part)
        m = jnp.max(top, axis=1, keepdims=True)
        total = None
        o = None
        for k in range(0, LISTED, 2):
            p = jnp.exp2((sc[:, k * 128 : (k + 2) * 128] - m) * scale)
            t = p[:, :128] + p[:, 128:]
            total = t if total is None else total + t
            vv = jnp.concatenate([pool[idx[k], 1], pool[idx[k + 1], 1]], axis=0)
            po = jnp.dot(p.astype(BF16), vv, preferred_element_type=F32)
            o = po if o is None else o + po
        l = jnp.sum(total, axis=1, keepdims=True)
        out[rows(b), a * 128 : (a + 1) * 128] = (o / l).astype(BF16)
        return carry

    for a in range(HEADS):
        for d, first, n in OFFSETS:
            src = f8 if d == 8 else f - d

            def arrive(first=first, n=n, a=a):
                for i in range(n):
                    kv_copy(a, first + i, f8).wait_recv()

            if d == 8:
                arrive()
            else:
                pl.when((src >= 0) & (src < GROUPS))(arrive)
        lax.fori_loop(0, NBLK, functools.partial(attend, a), 0)

    lax.fori_loop(0, NBLK, drain, 0)
    for a in range(HEADS):
        for d, first, n in OFFSETS:
            dst, ok = target(d)

            def sent(first=first, n=n, a=a, dst=dst):
                for i in range(n):
                    kv_copy(a, first + i, f8).wait_send()

            if ok is None:
                sent()
            else:
                pl.when(ok)(sent)


def body(
    tokens,
    mask_block_frame,
    attended_key_blocks,
    frozen_query_key_value,
    query_key_value_down_weight,
    query_key_value_up_weight,
    frozen_output_weight,
    output_down_weight,
    output_up_weight,
):
    rows = tokens.shape[0]
    width = frozen_output_weight.shape[0]
    table = attended_key_blocks.T
    any_spec = pl.BlockSpec(memory_space=pl.ANY)
    vmem = pl.BlockSpec(memory_space=pltpu.VMEM)
    smem = pl.BlockSpec(memory_space=pltpu.SMEM)
    attention_result = pl.pallas_call(
        kernel,
        out_shape=jax.ShapeDtypeStruct((rows, width), BF16),
        in_specs=[any_spec, vmem, smem, smem, vmem, any_spec, any_spec, vmem],
        out_specs=vmem,
        scratch_shapes=[
            pltpu.VMEM((rows, MODEL_WIDTH), BF16),
            pltpu.VMEM((3, MODEL_WIDTH, width), BF16),
            pltpu.VMEM((3 * RANK, MODEL_WIDTH), BF16),
            pltpu.VMEM((3, 3 * RANK, width), BF16),
            pltpu.VMEM((rows, 128), F32),
            pltpu.VMEM((rows, 128), F32),
            pltpu.VMEM((NB, 128), jnp.int32),
            pltpu.SMEM((NB, 128), jnp.int32),
            pltpu.VMEM((3, BLOCK, width), F32),
            pltpu.VMEM((BLOCK, 3 * RANK), F32),
            pltpu.VMEM((HEADS, rows, 128), BF16),
            pltpu.VMEM((HEADS, NBLK, 2, BLOCK, 128), BF16),
            pltpu.VMEM((HEADS, SLOTS, 2, BLOCK, 128), BF16),
            pltpu.VMEM((NBLK + SLOTS, 2, BLOCK, 128), BF16),
            pltpu.VMEM((NBLK + SLOTS, 2, BLOCK, 128), BF16),
            pltpu.VMEM((NBLK + SLOTS, 2, BLOCK, 128), BF16),
            pltpu.VMEM((BLOCK, LISTED * BLOCK), F32),
            pltpu.SemaphoreType.DMA((3,)),
            pltpu.SemaphoreType.DMA((9, NBLK)),
            pltpu.SemaphoreType.DMA((9, NBLK)),
            pltpu.SemaphoreType.DMA((HEADS, SLOTS)),
            pltpu.SemaphoreType.DMA((HEADS, SLOTS)),
            pltpu.SemaphoreType.DMA,
        ],
        compiler_params=pltpu.CompilerParams(
            collective_id=0, has_side_effects=True, vmem_limit_bytes=62 * 1024 * 1024
        ),
    )(
        tokens,
        table,
        table,
        mask_block_frame,
        jnp.asarray(rope_constants()),
        frozen_query_key_value.transpose(1, 0, 2),
        query_key_value_down_weight.T,
        query_key_value_up_weight.transpose(1, 0, 2),
    )
    adapter_output = lax.psum(
        jnp.dot(attention_result, output_down_weight, preferred_element_type=F32).astype(BF16),
        "head",
    )
    partial_value = jnp.dot(attention_result, frozen_output_weight, preferred_element_type=F32)
    frozen_output = lax.psum_scatter(
        partial_value.astype(BF16), "head", scatter_dimension=1, tiled=True
    ).astype(F32)
    return (
        frozen_output + jnp.dot(adapter_output, output_up_weight, preferred_element_type=F32)
    ).astype(BF16)


def solution(mesh):
    return jax.shard_map(
        body,
        mesh=mesh,
        in_specs=(
            P("frame", "head"),
            P(),
            P(),
            P(None, None, "head"),
            P(),
            P(None, None, "head"),
            P("head", None),
            P("head", None),
            P(None, "head"),
        ),
        out_specs=P("frame", "head"),
        check_vma=False,
    )
```

```python
import functools
import math

import jax
import jax.numpy as jnp
import numpy as np
from jax import lax
from jax.experimental import pallas as pl
from jax.experimental.pallas import tpu as pltpu
from jax.sharding import PartitionSpec as P

MODEL_WIDTH = 5120
HEAD_SIZE = 128
BLOCK = 128
LISTED = 10
NBLK = 6
GROUPS = 16
NB = 96
RANK = 64
HEADS = 3
SHARD = 640
TIME_PAIRS = 22
SPACE_PAIRS = 42
N_HEAD = 8
MESH = pl.DeviceIdType.MESH
F32 = jnp.float32
BF16 = jnp.bfloat16

OFFSETS = ((1, 0, 4), (-1, 4, 4), (2, 8, 2), (-2, 10, 2), (3, 12, 1), (-3, 13, 1), (8, 14, 2))
SLOTS = 16


def rope_constants():
    lanes = np.zeros((8, 128), np.float64)
    t = 10000.0 ** (-np.arange(TIME_PAIRS) / TIME_PAIRS)
    s = 10000.0 ** (-np.arange(SPACE_PAIRS) / SPACE_PAIRS)
    lanes[0] = np.concatenate([t, t, s, s])
    lanes[1] = np.concatenate(
        [-np.ones(TIME_PAIRS), np.ones(TIME_PAIRS), -np.ones(SPACE_PAIRS), np.ones(SPACE_PAIRS)]
    )
    lanes[2, : 2 * TIME_PAIRS] = 1.0
    return lanes.astype(np.float32)


def sin_cos(x):
    turns = jnp.floor(x * (1.0 / (2.0 * math.pi)) + 0.5)
    c1 = 6.28125
    c2 = float(np.float32(np.round((2 * math.pi - c1) * 2**20) / 2**20))
    c3 = 2 * math.pi - c1 - c2
    r = ((x - turns * c1) - turns * c2) - turns * c3
    r2 = r * r
    s = jnp.full_like(r, -1.0 / math.factorial(19))
    for n in (17, 15, 13, 11, 9, 7, 5, 3, 1):
        s = s * r2 + (1.0 if n % 4 == 1 else -1.0) / math.factorial(n)
    c = jnp.full_like(r, 1.0 / math.factorial(20))
    for n in (18, 16, 14, 12, 10, 8, 6, 4, 2, 0):
        c = c * r2 + (1.0 if n % 4 == 0 else -1.0) / math.factorial(n)
    return s * r, c


def kernel(
    tok, tabv, tabs, mbf, consts, wq, dn, up, wo, od, ou,
    out, wog,
    xg, wv, dnv, upv, cosv, sinv, planv, plans, acc, accl, qv, own, sb, pool0, pool1, pool2, sc,
    wov, odl, odg, attg, oacc, lacc,
    loc_sem, ag_send, ag_recv, kv_send, kv_recv, plan_sem,
    wz_send, wz_recv, wr_send, wr_recv, at_send, at_recv,
):
    f = lax.axis_index("frame")
    h = lax.axis_index("head")
    z = h // 2
    core = h % 2
    up_h = ((z + 1) % 4) * 2 + core
    dn_h = ((z + 3) % 4) * 2 + core
    far_h = ((z + 2) % 4) * 2 + core
    other = z * 2 + (1 - core)
    f8 = (f + 8) % GROUPS
    y = f // 4
    x = f % 4
    x_up = y * 4 + (x + 1) % 4
    x_dn = y * 4 + (x + 3) % 4
    y_up = ((y + 1) % 4) * 4 + x
    y_dn = ((y + 3) % 4) * 4 + x
    pools = (pool0, pool1, pool2)

    def target(d):
        if d == 8:
            return f8, None
        dst = f + d
        return dst, (dst >= 0) & (dst < GROUPS)

    rows_all = pl.ds(0, NBLK * BLOCK)
    ld_tok = pltpu.make_async_copy(
        tok, xg.at[rows_all, pl.ds(pl.multiple_of(h * SHARD, 128), SHARD)], loc_sem.at[0]
    )
    ld_w = pltpu.make_async_copy(wq, wv, loc_sem.at[1])
    ld_dn = pltpu.make_async_copy(dn, dnv, loc_sem.at[2])
    ld_od = [
        pltpu.make_async_copy(od.at[:, a * 128 : (a + 1) * 128], odl.at[a], loc_sem.at[3 + a])
        for a in range(HEADS)
    ]
    ld_tok.start()
    for cp in ld_od:
        cp.start()
    ld_w.start()
    ld_dn.start()

    barrier = pltpu.get_barrier_semaphore()
    for j in range(1, N_HEAD):
        pl.semaphore_signal(barrier, inc=1, device_id=(f, (h + j) % N_HEAD), device_id_type=MESH)
    for ff in (x_up, x_dn, y_up, y_dn):
        pl.semaphore_signal(barrier, inc=1, device_id=(ff, h), device_id_type=MESH)
    for d, _, _ in OFFSETS:
        dst, ok = target(d)

        def greet(dst=dst):
            pl.semaphore_signal(barrier, inc=1, device_id=(dst, h), device_id_type=MESH)

        if ok is None:
            greet()
        else:
            pl.when(ok)(greet)
    count = N_HEAD - 1 + 4 + 1
    for d in (1, -1, 2, -2, 3, -3):
        count = count + ((f + d >= 0) & (f + d < GROUPS)).astype(jnp.int32)
    pl.semaphore_wait(barrier, count)

    def cols(hh):
        return pl.ds(pl.multiple_of(hh * SHARD, 128), SHARD)

    def rows(r, start=0, size=BLOCK):
        return pl.ds(pl.multiple_of(r * BLOCK + start, 64), size)

    def ag_copy(kind, r, src_h, dst_h, start=0, size=BLOCK, from_tok=False):
        dst = xg.at[rows(r, start, size), cols(src_h)]
        src = tok.at[rows(r, start, size), :] if from_tok else dst
        return pltpu.make_async_remote_copy(
            src_ref=src, dst_ref=dst, send_sem=ag_send.at[kind, r], recv_sem=ag_recv.at[kind, r],
            device_id=(f, dst_h), device_id_type=MESH,
        )

    def wz_copy(j):
        dst_h = (h + j) % N_HEAD
        mine = jnp.where(h < 4, 4 * y + x, 4 * x + y)
        part = pl.ds(pl.multiple_of(mine * 8, 8), 8)
        src = wo.at[:, part, pl.ds(pl.multiple_of(dst_h * SHARD, 128), SHARD)]
        dst = wog.at[:, h, part, :]
        if j == 0:
            return pltpu.make_async_copy(src, dst, wz_send.at[0])
        return pltpu.make_async_remote_copy(
            src_ref=src, dst_ref=dst, send_sem=wz_send.at[j], recv_sem=wz_recv.at[j],
            device_id=(f, dst_h), device_id_type=MESH,
        )

    def ring_copy(half, stage, kind):
        along_x = half == stage
        here = x if along_x else y
        fixed = y if along_x else x
        if stage == 0:
            size = 8
            at = fixed * 4 + (here + 3) % 4 if kind == 2 else fixed * 4 + (here + 1) % 4 if kind == 3 else fixed * 4 + here
        else:
            size = 32
            at = (here + 3) % 4 if kind == 2 else (here + 1) % 4 if kind == 3 else here
        part = pl.ds(pl.multiple_of(at * size, 8), size)
        lo = 4 * half + (2 if kind == 3 else 0)
        n = 4 if kind < 2 else 2
        ref = wog.at[:, lo : lo + n, part, :]
        plus = kind in (0, 2)
        dst = (x_up if plus else x_dn) if along_x else (y_up if plus else y_dn)
        return pltpu.make_async_remote_copy(
            src_ref=ref, dst_ref=ref, send_sem=wr_send.at[half * 2 + stage, kind],
            recv_sem=wr_recv.at[half * 2 + stage, kind],
            device_id=(dst, h), device_id_type=MESH,
        )

    def weights_step(i):
        if i == 0:
            wz_copy(0).wait()
            for j in range(1, N_HEAD):
                wz_copy(j).wait_recv()
            for half in range(2):
                ring_copy(half, 0, 0).start()
                ring_copy(half, 0, 1).start()
        elif i == 1 or i == 3:
            for half in range(2):
                for kind in range(2):
                    ring_copy(half, i // 2, kind).wait_recv()
                    ring_copy(half, i // 2, kind + 2).start()
        else:
            for half in range(2):
                for kind in range(2, 4):
                    ring_copy(half, i // 2 - 1, kind).wait_recv()
            if i == 2:
                for half in range(2):
                    ring_copy(half, 1, 0).start()
                    ring_copy(half, 1, 1).start()

    def lanes(hh):
        return pl.ds(pl.multiple_of(hh * 128, 128), 128)

    def column_ring(view, i, src=None):
        def cp(kind, src_h, dst_h, half=None):
            dst = view(src_h, half)
            return pltpu.make_async_remote_copy(
                src_ref=src if src is not None and kind < 3 else dst, dst_ref=dst,
                send_sem=at_send.at[kind, i], recv_sem=at_recv.at[kind, i],
                device_id=(f, dst_h), device_id_type=MESH,
            )

        return (
            cp(0, h, up_h), cp(1, h, dn_h), cp(2, h, other),
            cp(3, dn_h, up_h, 0), cp(4, up_h, dn_h, 1),
            cp(5, dn_h, other), cp(6, up_h, other),
            cp(7, far_h, other, 0), cp(8, far_h, other, 1),
        )

    def advance(ring):
        ring[0].wait_recv()
        ring[3].start()
        ring[5].start()
        ring[1].wait_recv()
        ring[4].start()
        ring[6].start()

    def spread(ring):
        ring[3].wait_recv()
        ring[7].start()
        ring[4].wait_recv()
        ring[8].start()

    def settle(ring):
        for i in (2, 5, 6, 7, 8):
            ring[i].wait_recv()

    HALF = BLOCK // 2
    def own_up(r):
        return ag_copy(0, r, h, up_h, from_tok=True)

    def own_dn(r):
        return ag_copy(1, r, h, dn_h, from_tok=True)

    def own_other(r):
        return ag_copy(2, r, h, other, from_tok=True)

    def relay_up(r):
        return ag_copy(3, r, dn_h, up_h, 0, HALF)

    def relay_dn(r):
        return ag_copy(4, r, up_h, dn_h, HALF, HALF)

    def share_dn(r):
        return ag_copy(5, r, dn_h, other)

    def share_up(r):
        return ag_copy(6, r, up_h, other)

    def share_far0(r):
        return ag_copy(7, r, far_h, other, 0, HALF)

    def share_far1(r):
        return ag_copy(8, r, far_h, other, HALF, HALF)

    def start_own(r):
        own_up(r).start()
        own_dn(r).start()
        own_other(r).start()

    start_own(0)
    for j in range(N_HEAD):
        wz_copy(j).start()
    start_own(1)

    tab = tabv[...]
    gi = lax.broadcasted_iota(jnp.int32, (NB, NB), 0)
    ri = lax.broadcasted_iota(jnp.int32, (NB, NB), 1)
    member = jnp.zeros((NB, NB), F32)
    for k in range(LISTED):
        member = jnp.maximum(member, (jnp.broadcast_to(tab[k : k + 1, :], (NB, NB)) == gi).astype(F32))
    rq = lax.broadcasted_iota(jnp.int32, (NB, 128), 0)
    qq = lax.broadcasted_iota(jnp.int32, (NB, 128), 1)
    in_group = ((rq * 43) >> 8 == qq).astype(F32)
    used = (jnp.dot(member, in_group, preferred_element_type=F32) > 0.5).astype(F32)
    lower = (((gi * 43) >> 8 == (ri * 43) >> 8) & (ri < gi)).astype(F32)
    rank = jnp.dot(lower, used, preferred_element_type=F32)
    code = jnp.where(used > 0.5, rank, -1.0)
    mine = jnp.sum(jnp.where(qq == f, rank, 0.0), axis=1, keepdims=True)
    delta = ((rq * 43) >> 8) - f
    base = jnp.zeros((NB, 128), F32)
    for d, slot, _ in OFFSETS:
        hit = (delta == -d) if d != 8 else ((delta == 8) | (delta == -8))
        base = jnp.where(hit, float(NBLK + slot), base)
    place = jnp.where(delta == 0, (rq - NBLK * f).astype(F32), base + mine)
    planv[...] = jnp.where(qq == 127, place, code).astype(jnp.int32)
    plan_cp = pltpu.make_async_copy(planv, plans, plan_sem)
    plan_cp.start()

    freq = consts[0:1, :]
    sign = consts[1:2, :]
    timed = consts[2:3, :] > 0.5
    inner = lax.broadcasted_iota(jnp.int32, (BLOCK, 128), 0)

    def table(b, carry):
        g = f * NBLK + b
        fr = mbf[g]

        def tally(i, n):
            return n + (mbf[i] < fr).astype(jnp.int32)

        first = lax.fori_loop(0, NB, tally, jnp.int32(0))
        pos = ((g - first) * BLOCK + inner).astype(F32)
        frame_pos = jnp.zeros((BLOCK, 128), F32) + fr.astype(F32)
        angle = jnp.where(jnp.broadcast_to(timed, (BLOCK, 128)), frame_pos, pos) * freq
        sn, cs = sin_cos(angle)
        cosv[rows(b), :] = cs
        sinv[rows(b), :] = sn * sign
        return carry

    lax.fori_loop(0, NBLK, table, 0)

    upv[...] = jnp.zeros_like(upv)
    for s in range(3):
        upv[s, s * RANK : (s + 1) * RANK, :] = up[s]

    ld_tok.wait()
    ld_w.wait()
    ld_dn.wait()
    plan_cp.wait()

    lane = lax.broadcasted_iota(jnp.int32, (BLOCK, 128), 1)

    def rope(u, cs, sn):
        rot = jnp.where(
            lane < TIME_PAIRS,
            pltpu.roll(u, 128 - TIME_PAIRS, 1),
            jnp.where(
                lane < 2 * TIME_PAIRS,
                pltpu.roll(u, TIME_PAIRS, 1),
                jnp.where(
                    lane < 2 * TIME_PAIRS + SPACE_PAIRS,
                    pltpu.roll(u, 128 - SPACE_PAIRS, 1),
                    pltpu.roll(u, SPACE_PAIRS, 1),
                ),
            ),
        )
        return u * cs + rot * sn

    KC = 1280

    def compute(r):
        def step(k, carry):
            ks = pl.ds(pl.multiple_of(k * KC, 128), KC)
            xk = xg[rows(r), ks]
            keep = (k > 0).astype(F32)
            for s in range(3):
                part = jnp.dot(xk, wv[s, ks, :], preferred_element_type=F32)
                acc[s] = jnp.where(k > 0, acc[s], 0.0) + part
            low = lax.dot_general(xk, dnv[:, ks], (((1,), (1,)), ((), ())), preferred_element_type=F32)
            accl[...] = jnp.where(k > 0, accl[...], 0.0) + low
            return carry

        lax.fori_loop(0, MODEL_WIDTH // KC, step, 0)
        low = accl[...].astype(BF16)
        cs = cosv[rows(r), :]
        sn = sinv[rows(r), :]
        for s in range(3):
            y = acc[s] + jnp.dot(low, upv[s], preferred_element_type=F32)
            for a in range(HEADS):
                u = y[:, a * 128 : (a + 1) * 128]
                if s == 0:
                    qv[a, rows(r), :] = rope(u, cs, sn).astype(BF16)
                elif s == 1:
                    k = rope(u, cs, sn).astype(BF16)
                    own[a, r, 0] = k
                    pools[a][r, 0] = k
                else:
                    v = u.astype(BF16)
                    own[a, r, 1] = v
                    pools[a][r, 1] = v

    def kv_copy(a, slot, dst):
        return pltpu.make_async_remote_copy(
            src_ref=sb.at[a, slot], dst_ref=pools[a].at[NBLK + slot],
            send_sem=kv_send.at[a, slot], recv_sem=kv_recv.at[a, slot],
            device_id=(dst, h), device_id_type=MESH,
        )

    def send_slot(d, slot, rank_of):
        dst, ok = target(d)

        def go():
            idx = jnp.int32(0)
            for b in range(1, NBLK):
                idx = jnp.where(plans[f * NBLK + b, dst] == rank_of, b, idx)
            for a in range(HEADS):
                sb[a, slot] = own[a, idx]
                kv_copy(a, slot, dst).start()

        if ok is None:
            go()
        else:
            pl.when(ok)(go)

    def finish(r):
        relay_up(r).wait_recv()
        share_far0(r).start()
        relay_dn(r).wait_recv()
        share_far1(r).start()
        own_other(r).wait_recv()
        share_dn(r).wait_recv()
        share_up(r).wait_recv()
        share_far0(r).wait_recv()
        share_far1(r).wait_recv()
        compute(r)
        for ready in range(NBLK):
            slots = [
                (d, first + i, i)
                for d, first, n in OFFSETS
                for i in range(n)
                if NBLK - n + i == ready
            ]
            if slots:

                @pl.when(r == ready)
                def _():
                    for d, slot, i in slots:
                        send_slot(d, slot, i)

    def ring(r, carry):
        own_up(r).wait_recv()
        relay_up(r).start()
        share_dn(r).start()
        own_dn(r).wait_recv()
        relay_dn(r).start()
        share_up(r).start()

        @pl.when(r + 2 < NBLK)
        def _():
            start_own(r + 2)

        for i in range(4):

            @pl.when(r == i + 2)
            def _():
                weights_step(i)

        @pl.when(r > 0)
        def _():
            finish(r - 1)

        return carry

    lax.fori_loop(0, NBLK, ring, 0)
    od_ring = column_ring(
        lambda hh, half: odg.at[:, slice(0, RANK) if half is None else slice(32 * half, 32 * half + 32), lanes(hh)],
        NBLK, odl,
    )
    for cp in ld_od:
        cp.wait()
    for a in range(HEADS):
        odg[a, :, lanes(h)] = odl[a]
    for i in range(3):
        od_ring[i].start()
    finish(NBLK - 1)
    advance(od_ring)
    spread(od_ring)
    settle(od_ring)

    def drain(r, carry):
        for cp in (own_up, own_dn, own_other, relay_up, relay_dn, share_dn, share_up, share_far0, share_far1):
            cp(r).wait_send()
        return carry

    scale = math.log2(math.e) / math.sqrt(HEAD_SIZE)

    def attend(a, b, carry):
        pool = pools[a]
        q = qv[a, rows(b), :]
        idx = [
            jnp.clip(plans[tabs[k, f * NBLK + b], 127], 0, NBLK + SLOTS - 1) for k in range(LISTED)
        ]
        top = None
        for k in range(0, LISTED, 2):
            kk = jnp.concatenate([pool[idx[k], 0], pool[idx[k + 1], 0]], axis=0)
            s = lax.dot_general(q, kk, (((1,), (1,)), ((), ())), preferred_element_type=F32)
            sc[:, k * 128 : (k + 2) * 128] = s
            part = jnp.maximum(s[:, :128], s[:, 128:])
            top = part if top is None else jnp.maximum(top, part)
        m = jnp.max(top, axis=1, keepdims=True)
        total = None
        o = None
        for k in range(0, LISTED, 2):
            p = jnp.exp2((sc[:, k * 128 : (k + 2) * 128] - m) * scale)
            t = p[:, :128] + p[:, 128:]
            total = t if total is None else total + t
            vv = jnp.concatenate([pool[idx[k], 1], pool[idx[k + 1], 1]], axis=0)
            po = jnp.dot(p.astype(BF16), vv, preferred_element_type=F32)
            o = po if o is None else o + po
        l = jnp.sum(total, axis=1, keepdims=True)
        attg[a, rows(b), lanes(h)] = (o / l).astype(BF16)
        return carry

    PART = 3 * BLOCK

    def at_ring(i):
        a, c = i // 2, i % 2

        def view(hh, half):
            start = c * PART + (0 if half is None else half * (PART // 2))
            return attg.at[a, start : start + (PART if half is None else PART // 2), lanes(hh)]

        return column_ring(view, i)

    def project(i):
        a, c = i // 2, i % 2

        def go(b, carry):
            xa = attg[a, rows(b), :]
            part = jnp.dot(xa, wov[a].reshape(N_HEAD * 128, SHARD), preferred_element_type=F32)
            low = lax.dot_general(xa, odg[a], (((1,), (1,)), ((), ())), preferred_element_type=F32)
            if a == 0:
                oacc[rows(b), :] = part
                lacc[rows(b), :] = low
            elif a == 1:
                oacc[rows(b), :] += part
                lacc[rows(b), :] += low
            else:
                low = (lacc[rows(b), :] + low).astype(BF16)
                total = oacc[rows(b), :] + part
                out[rows(b), :] = (
                    total + jnp.dot(low, ou[...], preferred_element_type=F32)
                ).astype(BF16)
            return carry

        lax.fori_loop(c * 3, c * 3 + 3, go, 0)

    ld_wo = pltpu.make_async_copy(wog, wov, loc_sem.at[6])
    rings = [at_ring(i) for i in range(2 * HEADS)]
    for i in range(2 * HEADS):
        a, c = i // 2, i % 2
        if c == 0:
            for d, first, n in OFFSETS:
                src = f8 if d == 8 else f - d

                def arrive(first=first, n=n, a=a):
                    for j in range(n):
                        kv_copy(a, first + j, f8).wait_recv()

                if d == 8:
                    arrive()
                else:
                    pl.when((src >= 0) & (src < GROUPS))(arrive)
        lax.fori_loop(c * 3, c * 3 + 3, functools.partial(attend, a), 0)
        for j in range(3):
            rings[i][j].start()
        if i == 0:
            weights_step(4)
            ld_wo.start()
        if i >= 1:
            advance(rings[i - 1])
        if i >= 2:
            spread(rings[i - 2])
        if i == 3:
            ld_wo.wait()
        if i >= 3:
            settle(rings[i - 3])
            project(i - 3)
    advance(rings[5])
    spread(rings[4])
    settle(rings[3])
    project(3)
    spread(rings[5])
    settle(rings[4])
    project(4)
    settle(rings[5])
    project(5)

    for ring in rings + [od_ring]:
        for cp in ring:
            cp.wait_send()
    for j in range(1, N_HEAD):
        wz_copy(j).wait_send()
    for half in range(2):
        for stage in range(2):
            for kind in range(4):
                ring_copy(half, stage, kind).wait_send()
    lax.fori_loop(0, NBLK, drain, 0)
    for a in range(HEADS):
        for d, first, n in OFFSETS:
            dst, ok = target(d)

            def sent(first=first, n=n, a=a, dst=dst):
                for i in range(n):
                    kv_copy(a, first + i, f8).wait_send()

            if ok is None:
                sent()
            else:
                pl.when(ok)(sent)


def body(
    tokens,
    mask_block_frame,
    attended_key_blocks,
    frozen_query_key_value,
    query_key_value_down_weight,
    query_key_value_up_weight,
    frozen_output_weight,
    output_down_weight,
    output_up_weight,
):
    rows = tokens.shape[0]
    width = frozen_output_weight.shape[0]
    table = attended_key_blocks.T
    any_spec = pl.BlockSpec(memory_space=pl.ANY)
    vmem = pl.BlockSpec(memory_space=pltpu.VMEM)
    smem = pl.BlockSpec(memory_space=pltpu.SMEM)
    out, _ = pl.pallas_call(
        kernel,
        out_shape=(
            jax.ShapeDtypeStruct((rows, SHARD), BF16),
            jax.ShapeDtypeStruct((HEADS, N_HEAD, 128, SHARD), BF16),
        ),
        in_specs=[
            any_spec, vmem, smem, smem, vmem, any_spec, any_spec, vmem, any_spec, any_spec, vmem
        ],
        out_specs=(vmem, any_spec),
        scratch_shapes=[
            pltpu.VMEM((rows, MODEL_WIDTH), BF16),
            pltpu.VMEM((3, MODEL_WIDTH, width), BF16),
            pltpu.VMEM((3 * RANK, MODEL_WIDTH), BF16),
            pltpu.VMEM((3, 3 * RANK, width), BF16),
            pltpu.VMEM((rows, 128), F32),
            pltpu.VMEM((rows, 128), F32),
            pltpu.VMEM((NB, 128), jnp.int32),
            pltpu.SMEM((NB, 128), jnp.int32),
            pltpu.VMEM((3, BLOCK, width), F32),
            pltpu.VMEM((BLOCK, 3 * RANK), F32),
            pltpu.VMEM((HEADS, rows, 128), BF16),
            pltpu.VMEM((HEADS, NBLK, 2, BLOCK, 128), BF16),
            pltpu.VMEM((HEADS, SLOTS, 2, BLOCK, 128), BF16),
            pltpu.VMEM((NBLK + SLOTS, 2, BLOCK, 128), BF16),
            pltpu.VMEM((NBLK + SLOTS, 2, BLOCK, 128), BF16),
            pltpu.VMEM((NBLK + SLOTS, 2, BLOCK, 128), BF16),
            pltpu.VMEM((BLOCK, LISTED * BLOCK), F32),
            pltpu.VMEM((HEADS, N_HEAD, 128, SHARD), BF16),
            pltpu.VMEM((HEADS, RANK, 128), BF16),
            pltpu.VMEM((HEADS, RANK, N_HEAD * 128), BF16),
            pltpu.VMEM((HEADS, rows, N_HEAD * 128), BF16),
            pltpu.VMEM((rows, SHARD), F32),
            pltpu.VMEM((rows, RANK), F32),
            pltpu.SemaphoreType.DMA((7,)),
            pltpu.SemaphoreType.DMA((9, NBLK)),
            pltpu.SemaphoreType.DMA((9, NBLK)),
            pltpu.SemaphoreType.DMA((HEADS, SLOTS)),
            pltpu.SemaphoreType.DMA((HEADS, SLOTS)),
            pltpu.SemaphoreType.DMA,
            pltpu.SemaphoreType.DMA((N_HEAD,)),
            pltpu.SemaphoreType.DMA((N_HEAD,)),
            pltpu.SemaphoreType.DMA((4, 4)),
            pltpu.SemaphoreType.DMA((4, 4)),
            pltpu.SemaphoreType.DMA((9, NBLK + 1)),
            pltpu.SemaphoreType.DMA((9, NBLK + 1)),
        ],
        compiler_params=pltpu.CompilerParams(
            collective_id=0, has_side_effects=True, vmem_limit_bytes=62 * 1024 * 1024
        ),
    )(
        tokens,
        table,
        table,
        mask_block_frame,
        jnp.asarray(rope_constants()),
        frozen_query_key_value.transpose(1, 0, 2),
        query_key_value_down_weight.T,
        query_key_value_up_weight.transpose(1, 0, 2),
        frozen_output_weight.reshape(HEADS, 128, MODEL_WIDTH),
        output_down_weight.T,
        output_up_weight,
    )
    return out


def solution(mesh):
    return jax.shard_map(
        body,
        mesh=mesh,
        in_specs=(
            P("frame", "head"),
            P(),
            P(),
            P(None, None, "head"),
            P(),
            P(None, None, "head"),
            P("head", None),
            P("head", None),
            P(None, "head"),
        ),
        out_specs=P("frame", "head"),
        check_vma=False,
    )
```

```python
import functools
import math

import jax
import jax.numpy as jnp
import numpy as np
from jax import lax
from jax.experimental import pallas as pl
from jax.experimental.pallas import tpu as pltpu
from jax.sharding import PartitionSpec as P

MODEL_WIDTH = 5120
HEAD_SIZE = 128
BLOCK = 128
LISTED = 10
NBLK = 6
GROUPS = 16
NB = 96
RANK = 64
HEADS = 3
SHARD = 640
TIME_PAIRS = 22
SPACE_PAIRS = 42
N_HEAD = 8
MESH = pl.DeviceIdType.MESH
F32 = jnp.float32
BF16 = jnp.bfloat16

OFFSETS = ((1, 0, 4), (-1, 4, 4), (2, 8, 2), (-2, 10, 2), (3, 12, 1), (-3, 13, 1), (8, 14, 2))
SLOTS = 16


def rope_constants():
    lanes = np.zeros((8, 128), np.float64)
    t = 10000.0 ** (-np.arange(TIME_PAIRS) / TIME_PAIRS)
    s = 10000.0 ** (-np.arange(SPACE_PAIRS) / SPACE_PAIRS)
    lanes[0] = np.concatenate([t, t, s, s])
    lanes[1] = np.concatenate(
        [-np.ones(TIME_PAIRS), np.ones(TIME_PAIRS), -np.ones(SPACE_PAIRS), np.ones(SPACE_PAIRS)]
    )
    lanes[2, : 2 * TIME_PAIRS] = 1.0
    return lanes.astype(np.float32)


def sin_cos(x):
    turns = jnp.floor(x * (1.0 / (2.0 * math.pi)) + 0.5)
    c1 = 6.28125
    c2 = float(np.float32(np.round((2 * math.pi - c1) * 2**20) / 2**20))
    c3 = 2 * math.pi - c1 - c2
    r = ((x - turns * c1) - turns * c2) - turns * c3
    r2 = r * r
    s = jnp.full_like(r, -1.0 / math.factorial(19))
    for n in (17, 15, 13, 11, 9, 7, 5, 3, 1):
        s = s * r2 + (1.0 if n % 4 == 1 else -1.0) / math.factorial(n)
    c = jnp.full_like(r, 1.0 / math.factorial(20))
    for n in (18, 16, 14, 12, 10, 8, 6, 4, 2, 0):
        c = c * r2 + (1.0 if n % 4 == 0 else -1.0) / math.factorial(n)
    return s * r, c


def kernel(
    tok, tabv, tabs, mbf, consts, wq, dn, up, wo, od, ou,
    out, wog,
    xg, wv, dnv, upv, cosv, sinv, planv, plans, acc, accl, qv, own, sb, pool0, pool1, pool2, sc,
    wov, odl, odg, attg, oacc, lacc,
    loc_sem, ag_send, ag_recv, kv_send, kv_recv, plan_sem,
    wz_send, wz_recv, wr_send, wr_recv, at_send, at_recv,
):
    f = lax.axis_index("frame")
    h = lax.axis_index("head")
    z = h // 2
    core = h % 2
    up_h = ((z + 1) % 4) * 2 + core
    dn_h = ((z + 3) % 4) * 2 + core
    far_h = ((z + 2) % 4) * 2 + core
    other = z * 2 + (1 - core)
    f8 = (f + 8) % GROUPS
    y = f // 4
    x = f % 4
    x_up = y * 4 + (x + 1) % 4
    x_dn = y * 4 + (x + 3) % 4
    y_up = ((y + 1) % 4) * 4 + x
    y_dn = ((y + 3) % 4) * 4 + x
    pools = (pool0, pool1, pool2)

    def target(d):
        if d == 8:
            return f8, None
        dst = f + d
        return dst, (dst >= 0) & (dst < GROUPS)

    rows_all = pl.ds(0, NBLK * BLOCK)
    ld_tok = pltpu.make_async_copy(
        tok, xg.at[rows_all, pl.ds(pl.multiple_of(h * SHARD, 128), SHARD)], loc_sem.at[0]
    )
    ld_w = pltpu.make_async_copy(wq, wv, loc_sem.at[1])
    ld_dn = pltpu.make_async_copy(dn, dnv, loc_sem.at[2])
    ld_od = [
        pltpu.make_async_copy(od.at[:, a * 128 : (a + 1) * 128], odl.at[a], loc_sem.at[3 + a])
        for a in range(HEADS)
    ]
    ld_tok.start()
    for cp in ld_od:
        cp.start()
    ld_w.start()
    ld_dn.start()

    barrier = pltpu.get_barrier_semaphore()
    for j in range(1, N_HEAD):
        pl.semaphore_signal(barrier, inc=1, device_id=(f, (h + j) % N_HEAD), device_id_type=MESH)
    for ff in (x_up, x_dn, y_up, y_dn):
        pl.semaphore_signal(barrier, inc=1, device_id=(ff, h), device_id_type=MESH)
    for d, _, _ in OFFSETS:
        dst, ok = target(d)

        def greet(dst=dst):
            pl.semaphore_signal(barrier, inc=1, device_id=(dst, h), device_id_type=MESH)

        if ok is None:
            greet()
        else:
            pl.when(ok)(greet)
    count = N_HEAD - 1 + 4 + 1
    for d in (1, -1, 2, -2, 3, -3):
        count = count + ((f + d >= 0) & (f + d < GROUPS)).astype(jnp.int32)
    pl.semaphore_wait(barrier, count)

    def cols(hh):
        return pl.ds(pl.multiple_of(hh * SHARD, 128), SHARD)

    def rows(r, start=0, size=BLOCK):
        return pl.ds(pl.multiple_of(r * BLOCK + start, 64), size)

    def ag_copy(kind, r, src_h, dst_h, start=0, size=BLOCK, from_tok=False):
        dst = xg.at[rows(r, start, size), cols(src_h)]
        src = tok.at[rows(r, start, size), :] if from_tok else dst
        return pltpu.make_async_remote_copy(
            src_ref=src, dst_ref=dst, send_sem=ag_send.at[kind, r], recv_sem=ag_recv.at[kind, r],
            device_id=(f, dst_h), device_id_type=MESH,
        )

    def wz_copy(j):
        dst_h = (h + j) % N_HEAD
        mine = jnp.where(h < 4, 4 * y + x, 4 * x + y)
        part = pl.ds(pl.multiple_of(mine * 8, 8), 8)
        src = wo.at[:, part, pl.ds(pl.multiple_of(dst_h * SHARD, 128), SHARD)]
        dst = wog.at[:, h, part, :]
        if j == 0:
            return pltpu.make_async_copy(src, dst, wz_send.at[0])
        return pltpu.make_async_remote_copy(
            src_ref=src, dst_ref=dst, send_sem=wz_send.at[j], recv_sem=wz_recv.at[j],
            device_id=(f, dst_h), device_id_type=MESH,
        )

    def ring_copy(half, stage, kind):
        along_x = half == stage
        here = x if along_x else y
        fixed = y if along_x else x
        if stage == 0:
            size = 8
            at = fixed * 4 + (here + 3) % 4 if kind == 2 else fixed * 4 + (here + 1) % 4 if kind == 3 else fixed * 4 + here
        else:
            size = 32
            at = (here + 3) % 4 if kind == 2 else (here + 1) % 4 if kind == 3 else here
        part = pl.ds(pl.multiple_of(at * size, 8), size)
        lo = 4 * half + (2 if kind == 3 else 0)
        n = 4 if kind < 2 else 2
        ref = wog.at[:, lo : lo + n, part, :]
        plus = kind in (0, 2)
        dst = (x_up if plus else x_dn) if along_x else (y_up if plus else y_dn)
        return pltpu.make_async_remote_copy(
            src_ref=ref, dst_ref=ref, send_sem=wr_send.at[half * 2 + stage, kind],
            recv_sem=wr_recv.at[half * 2 + stage, kind],
            device_id=(dst, h), device_id_type=MESH,
        )

    def weights_step(i):
        if i == 0:
            wz_copy(0).wait()
            for j in range(1, N_HEAD):
                wz_copy(j).wait_recv()
            for half in range(2):
                ring_copy(half, 0, 0).start()
                ring_copy(half, 0, 1).start()
        elif i == 1 or i == 3:
            for half in range(2):
                for kind in range(2):
                    ring_copy(half, i // 2, kind).wait_recv()
                    ring_copy(half, i // 2, kind + 2).start()
        else:
            for half in range(2):
                for kind in range(2, 4):
                    ring_copy(half, i // 2 - 1, kind).wait_recv()
            if i == 2:
                for half in range(2):
                    ring_copy(half, 1, 0).start()
                    ring_copy(half, 1, 1).start()

    def lanes(hh):
        return pl.ds(pl.multiple_of(hh * 128, 128), 128)

    def column_ring(view, i, src=None):
        def cp(kind, src_h, dst_h, half=None):
            dst = view(src_h, half)
            return pltpu.make_async_remote_copy(
                src_ref=src if src is not None and kind < 3 else dst, dst_ref=dst,
                send_sem=at_send.at[kind, i], recv_sem=at_recv.at[kind, i],
                device_id=(f, dst_h), device_id_type=MESH,
            )

        return (
            cp(0, h, up_h), cp(1, h, dn_h), cp(2, h, other),
            cp(3, dn_h, up_h, 0), cp(4, up_h, dn_h, 1),
            cp(5, dn_h, other), cp(6, up_h, other),
            cp(7, far_h, other, 0), cp(8, far_h, other, 1),
        )

    def advance(ring):
        ring[0].wait_recv()
        ring[3].start()
        ring[5].start()
        ring[1].wait_recv()
        ring[4].start()
        ring[6].start()

    def spread(ring):
        ring[3].wait_recv()
        ring[7].start()
        ring[4].wait_recv()
        ring[8].start()

    def settle(ring):
        for i in (2, 5, 6, 7, 8):
            ring[i].wait_recv()

    HALF = BLOCK // 2
    def own_up(r):
        return ag_copy(0, r, h, up_h, from_tok=True)

    def own_dn(r):
        return ag_copy(1, r, h, dn_h, from_tok=True)

    def own_other(r):
        return ag_copy(2, r, h, other, from_tok=True)

    def relay_up(r):
        return ag_copy(3, r, dn_h, up_h, 0, HALF)

    def relay_dn(r):
        return ag_copy(4, r, up_h, dn_h, HALF, HALF)

    def share_dn(r):
        return ag_copy(5, r, dn_h, other)

    def share_up(r):
        return ag_copy(6, r, up_h, other)

    def share_far0(r):
        return ag_copy(7, r, far_h, other, 0, HALF)

    def share_far1(r):
        return ag_copy(8, r, far_h, other, HALF, HALF)

    def start_own(r):
        own_up(r).start()
        own_dn(r).start()
        own_other(r).start()

    for j in range(N_HEAD):
        wz_copy(j).start()
    start_own(0)
    start_own(1)

    tab = tabv[...]
    gi = lax.broadcasted_iota(jnp.int32, (NB, NB), 0)
    ri = lax.broadcasted_iota(jnp.int32, (NB, NB), 1)
    member = jnp.zeros((NB, NB), F32)
    for k in range(LISTED):
        member = jnp.maximum(member, (jnp.broadcast_to(tab[k : k + 1, :], (NB, NB)) == gi).astype(F32))
    rq = lax.broadcasted_iota(jnp.int32, (NB, 128), 0)
    qq = lax.broadcasted_iota(jnp.int32, (NB, 128), 1)
    in_group = ((rq * 43) >> 8 == qq).astype(F32)
    used = (jnp.dot(member, in_group, preferred_element_type=F32) > 0.5).astype(F32)
    lower = (((gi * 43) >> 8 == (ri * 43) >> 8) & (ri < gi)).astype(F32)
    rank = jnp.dot(lower, used, preferred_element_type=F32)
    code = jnp.where(used > 0.5, rank, -1.0)
    mine = jnp.sum(jnp.where(qq == f, rank, 0.0), axis=1, keepdims=True)
    delta = ((rq * 43) >> 8) - f
    base = jnp.zeros((NB, 128), F32)
    for d, slot, _ in OFFSETS:
        hit = (delta == -d) if d != 8 else ((delta == 8) | (delta == -8))
        base = jnp.where(hit, float(NBLK + slot), base)
    place = jnp.where(delta == 0, (rq - NBLK * f).astype(F32), base + mine)
    planv[...] = jnp.where(qq == 127, place, code).astype(jnp.int32)
    plan_cp = pltpu.make_async_copy(planv, plans, plan_sem)
    plan_cp.start()

    freq = consts[0:1, :]
    sign = consts[1:2, :]
    timed = consts[2:3, :] > 0.5
    inner = lax.broadcasted_iota(jnp.int32, (BLOCK, 128), 0)

    def table(b, carry):
        g = f * NBLK + b
        fr = mbf[g]

        def tally(i, n):
            return n + (mbf[i] < fr).astype(jnp.int32)

        first = lax.fori_loop(0, NB, tally, jnp.int32(0))
        pos = ((g - first) * BLOCK + inner).astype(F32)
        frame_pos = jnp.zeros((BLOCK, 128), F32) + fr.astype(F32)
        angle = jnp.where(jnp.broadcast_to(timed, (BLOCK, 128)), frame_pos, pos) * freq
        sn, cs = sin_cos(angle)
        cosv[rows(b), :] = cs
        sinv[rows(b), :] = sn * sign
        return carry

    lax.fori_loop(0, NBLK, table, 0)

    upv[...] = jnp.zeros_like(upv)
    for s in range(3):
        upv[s, s * RANK : (s + 1) * RANK, :] = up[s]

    weights_step(0)
    ld_tok.wait()
    ld_w.wait()
    ld_dn.wait()
    plan_cp.wait()

    lane = lax.broadcasted_iota(jnp.int32, (BLOCK, 128), 1)

    def rope(u, cs, sn):
        rot = jnp.where(
            lane < TIME_PAIRS,
            pltpu.roll(u, 128 - TIME_PAIRS, 1),
            jnp.where(
                lane < 2 * TIME_PAIRS,
                pltpu.roll(u, TIME_PAIRS, 1),
                jnp.where(
                    lane < 2 * TIME_PAIRS + SPACE_PAIRS,
                    pltpu.roll(u, 128 - SPACE_PAIRS, 1),
                    pltpu.roll(u, SPACE_PAIRS, 1),
                ),
            ),
        )
        return u * cs + rot * sn

    KC = 1280

    def compute(r):
        def step(k, carry):
            ks = pl.ds(pl.multiple_of(k * KC, 128), KC)
            xk = xg[rows(r), ks]
            keep = (k > 0).astype(F32)
            for s in range(3):
                part = jnp.dot(xk, wv[s, ks, :], preferred_element_type=F32)
                acc[s] = jnp.where(k > 0, acc[s], 0.0) + part
            low = lax.dot_general(xk, dnv[:, ks], (((1,), (1,)), ((), ())), preferred_element_type=F32)
            accl[...] = jnp.where(k > 0, accl[...], 0.0) + low
            return carry

        lax.fori_loop(0, MODEL_WIDTH // KC, step, 0)
        low = accl[...].astype(BF16)
        cs = cosv[rows(r), :]
        sn = sinv[rows(r), :]
        for s in range(3):
            y = acc[s] + jnp.dot(low, upv[s], preferred_element_type=F32)
            for a in range(HEADS):
                u = y[:, a * 128 : (a + 1) * 128]
                if s == 0:
                    qv[a, rows(r), :] = rope(u, cs, sn).astype(BF16)
                elif s == 1:
                    k = rope(u, cs, sn).astype(BF16)
                    own[a, r, 0] = k
                    pools[a][r, 0] = k
                else:
                    v = u.astype(BF16)
                    own[a, r, 1] = v
                    pools[a][r, 1] = v

    def kv_copy(a, slot, dst):
        return pltpu.make_async_remote_copy(
            src_ref=sb.at[a, slot], dst_ref=pools[a].at[NBLK + slot],
            send_sem=kv_send.at[a, slot], recv_sem=kv_recv.at[a, slot],
            device_id=(dst, h), device_id_type=MESH,
        )

    def send_slot(d, slot, rank_of):
        dst, ok = target(d)

        def go():
            idx = jnp.int32(0)
            for b in range(1, NBLK):
                idx = jnp.where(plans[f * NBLK + b, dst] == rank_of, b, idx)
            for a in range(HEADS):
                sb[a, slot] = own[a, idx]
                kv_copy(a, slot, dst).start()

        if ok is None:
            go()
        else:
            pl.when(ok)(go)

    def finish(r):
        relay_up(r).wait_recv()
        share_far0(r).start()
        relay_dn(r).wait_recv()
        share_far1(r).start()
        own_other(r).wait_recv()
        share_dn(r).wait_recv()
        share_up(r).wait_recv()
        share_far0(r).wait_recv()
        share_far1(r).wait_recv()
        compute(r)
        for ready in range(NBLK):
            slots = [
                (d, first + i, i)
                for d, first, n in OFFSETS
                for i in range(n)
                if NBLK - n + i == ready
            ]
            if slots:

                @pl.when(r == ready)
                def _():
                    for d, slot, i in slots:
                        send_slot(d, slot, i)

    def ring(r, carry):
        own_up(r).wait_recv()
        relay_up(r).start()
        share_dn(r).start()
        own_dn(r).wait_recv()
        relay_dn(r).start()
        share_up(r).start()

        @pl.when(r + 2 < NBLK)
        def _():
            start_own(r + 2)

        for i, at in ((1, 1), (2, 2), (3, 4)):

            @pl.when(r == at)
            def _():
                weights_step(i)

        @pl.when(r > 0)
        def _():
            finish(r - 1)

        return carry

    lax.fori_loop(0, NBLK, ring, 0)
    od_ring = column_ring(
        lambda hh, half: odg.at[:, slice(0, RANK) if half is None else slice(32 * half, 32 * half + 32), lanes(hh)],
        NBLK, odl,
    )
    for cp in ld_od:
        cp.wait()
    for a in range(HEADS):
        odg[a, :, lanes(h)] = odl[a]
    for i in range(3):
        od_ring[i].start()
    finish(NBLK - 1)
    advance(od_ring)
    spread(od_ring)
    settle(od_ring)

    def drain(r, carry):
        for cp in (own_up, own_dn, own_other, relay_up, relay_dn, share_dn, share_up, share_far0, share_far1):
            cp(r).wait_send()
        return carry

    scale = math.log2(math.e) / math.sqrt(HEAD_SIZE)

    def attend(a, b, carry):
        pool = pools[a]
        q = qv[a, rows(b), :]
        idx = [
            jnp.clip(plans[tabs[k, f * NBLK + b], 127], 0, NBLK + SLOTS - 1) for k in range(LISTED)
        ]
        top = None
        for k in range(0, LISTED, 2):
            kk = jnp.concatenate([pool[idx[k], 0], pool[idx[k + 1], 0]], axis=0)
            s = lax.dot_general(q, kk, (((1,), (1,)), ((), ())), preferred_element_type=F32)
            sc[:, k * 128 : (k + 2) * 128] = s
            part = jnp.maximum(s[:, :128], s[:, 128:])
            top = part if top is None else jnp.maximum(top, part)
        m = jnp.max(top, axis=1, keepdims=True)
        total = None
        o = None
        for k in range(0, LISTED, 2):
            p = jnp.exp2((sc[:, k * 128 : (k + 2) * 128] - m) * scale)
            t = p[:, :128] + p[:, 128:]
            total = t if total is None else total + t
            vv = jnp.concatenate([pool[idx[k], 1], pool[idx[k + 1], 1]], axis=0)
            po = jnp.dot(p.astype(BF16), vv, preferred_element_type=F32)
            o = po if o is None else o + po
        l = jnp.sum(total, axis=1, keepdims=True)
        attg[a, rows(b), lanes(h)] = (o / l).astype(BF16)
        return carry

    PART = 3 * BLOCK

    def at_ring(i):
        a, c = i // 2, i % 2

        def view(hh, half):
            start = c * PART + (0 if half is None else half * (PART // 2))
            return attg.at[a, start : start + (PART if half is None else PART // 2), lanes(hh)]

        return column_ring(view, i)

    def project(i):
        a, c = i // 2, i % 2

        def go(b, carry):
            xa = attg[a, rows(b), :]
            part = jnp.dot(xa, wov[a].reshape(N_HEAD * 128, SHARD), preferred_element_type=F32)
            low = lax.dot_general(xa, odg[a], (((1,), (1,)), ((), ())), preferred_element_type=F32)
            if a == 0:
                oacc[rows(b), :] = part
                lacc[rows(b), :] = low
            elif a == 1:
                oacc[rows(b), :] += part
                lacc[rows(b), :] += low
            else:
                low = (lacc[rows(b), :] + low).astype(BF16)
                total = oacc[rows(b), :] + part
                out[rows(b), :] = (
                    total + jnp.dot(low, ou[...], preferred_element_type=F32)
                ).astype(BF16)
            return carry

        lax.fori_loop(c * 3, c * 3 + 3, go, 0)

    ld_wo = pltpu.make_async_copy(wog, wov, loc_sem.at[6])
    rings = [at_ring(i) for i in range(2 * HEADS)]
    for i in range(2 * HEADS):
        a, c = i // 2, i % 2
        if c == 0:
            for d, first, n in OFFSETS:
                src = f8 if d == 8 else f - d

                def arrive(first=first, n=n, a=a):
                    for j in range(n):
                        kv_copy(a, first + j, f8).wait_recv()

                if d == 8:
                    arrive()
                else:
                    pl.when((src >= 0) & (src < GROUPS))(arrive)
        lax.fori_loop(c * 3, c * 3 + 3, functools.partial(attend, a), 0)
        for j in range(3):
            rings[i][j].start()
        if i == 0:
            weights_step(4)
            ld_wo.start()
        if i >= 1:
            advance(rings[i - 1])
        if i >= 2:
            spread(rings[i - 2])
        if i == 3:
            ld_wo.wait()
        if i >= 3:
            settle(rings[i - 3])
            project(i - 3)
    advance(rings[5])
    spread(rings[4])
    settle(rings[3])
    project(3)
    spread(rings[5])
    settle(rings[4])
    project(4)
    settle(rings[5])
    project(5)

    for ring in rings + [od_ring]:
        for cp in ring:
            cp.wait_send()
    for j in range(1, N_HEAD):
        wz_copy(j).wait_send()
    for half in range(2):
        for stage in range(2):
            for kind in range(4):
                ring_copy(half, stage, kind).wait_send()
    lax.fori_loop(0, NBLK, drain, 0)
    for a in range(HEADS):
        for d, first, n in OFFSETS:
            dst, ok = target(d)

            def sent(first=first, n=n, a=a, dst=dst):
                for i in range(n):
                    kv_copy(a, first + i, f8).wait_send()

            if ok is None:
                sent()
            else:
                pl.when(ok)(sent)


def body(
    tokens,
    mask_block_frame,
    attended_key_blocks,
    frozen_query_key_value,
    query_key_value_down_weight,
    query_key_value_up_weight,
    frozen_output_weight,
    output_down_weight,
    output_up_weight,
):
    rows = tokens.shape[0]
    width = frozen_output_weight.shape[0]
    table = attended_key_blocks.T
    any_spec = pl.BlockSpec(memory_space=pl.ANY)
    vmem = pl.BlockSpec(memory_space=pltpu.VMEM)
    smem = pl.BlockSpec(memory_space=pltpu.SMEM)
    out, _ = pl.pallas_call(
        kernel,
        out_shape=(
            jax.ShapeDtypeStruct((rows, SHARD), BF16),
            jax.ShapeDtypeStruct((HEADS, N_HEAD, 128, SHARD), BF16),
        ),
        in_specs=[
            any_spec, vmem, smem, smem, vmem, any_spec, any_spec, vmem, any_spec, any_spec, vmem
        ],
        out_specs=(vmem, any_spec),
        scratch_shapes=[
            pltpu.VMEM((rows, MODEL_WIDTH), BF16),
            pltpu.VMEM((3, MODEL_WIDTH, width), BF16),
            pltpu.VMEM((3 * RANK, MODEL_WIDTH), BF16),
            pltpu.VMEM((3, 3 * RANK, width), BF16),
            pltpu.VMEM((rows, 128), F32),
            pltpu.VMEM((rows, 128), F32),
            pltpu.VMEM((NB, 128), jnp.int32),
            pltpu.SMEM((NB, 128), jnp.int32),
            pltpu.VMEM((3, BLOCK, width), F32),
            pltpu.VMEM((BLOCK, 3 * RANK), F32),
            pltpu.VMEM((HEADS, rows, 128), BF16),
            pltpu.VMEM((HEADS, NBLK, 2, BLOCK, 128), BF16),
            pltpu.VMEM((HEADS, SLOTS, 2, BLOCK, 128), BF16),
            pltpu.VMEM((NBLK + SLOTS, 2, BLOCK, 128), BF16),
            pltpu.VMEM((NBLK + SLOTS, 2, BLOCK, 128), BF16),
            pltpu.VMEM((NBLK + SLOTS, 2, BLOCK, 128), BF16),
            pltpu.VMEM((BLOCK, LISTED * BLOCK), F32),
            pltpu.VMEM((HEADS, N_HEAD, 128, SHARD), BF16),
            pltpu.VMEM((HEADS, RANK, 128), BF16),
            pltpu.VMEM((HEADS, RANK, N_HEAD * 128), BF16),
            pltpu.VMEM((HEADS, rows, N_HEAD * 128), BF16),
            pltpu.VMEM((rows, SHARD), F32),
            pltpu.VMEM((rows, RANK), F32),
            pltpu.SemaphoreType.DMA((7,)),
            pltpu.SemaphoreType.DMA((9, NBLK)),
            pltpu.SemaphoreType.DMA((9, NBLK)),
            pltpu.SemaphoreType.DMA((HEADS, SLOTS)),
            pltpu.SemaphoreType.DMA((HEADS, SLOTS)),
            pltpu.SemaphoreType.DMA,
            pltpu.SemaphoreType.DMA((N_HEAD,)),
            pltpu.SemaphoreType.DMA((N_HEAD,)),
            pltpu.SemaphoreType.DMA((4, 4)),
            pltpu.SemaphoreType.DMA((4, 4)),
            pltpu.SemaphoreType.DMA((9, NBLK + 1)),
            pltpu.SemaphoreType.DMA((9, NBLK + 1)),
        ],
        compiler_params=pltpu.CompilerParams(
            collective_id=0, has_side_effects=True, vmem_limit_bytes=62 * 1024 * 1024
        ),
    )(
        tokens,
        table,
        table,
        mask_block_frame,
        jnp.asarray(rope_constants()),
        frozen_query_key_value.transpose(1, 0, 2),
        query_key_value_down_weight.T,
        query_key_value_up_weight.transpose(1, 0, 2),
        frozen_output_weight.reshape(HEADS, 128, MODEL_WIDTH),
        output_down_weight.T,
        output_up_weight,
    )
    return out


def solution(mesh):
    return jax.shard_map(
        body,
        mesh=mesh,
        in_specs=(
            P("frame", "head"),
            P(),
            P(),
            P(None, None, "head"),
            P(),
            P(None, None, "head"),
            P("head", None),
            P("head", None),
            P(None, "head"),
        ),
        out_specs=P("frame", "head"),
        check_vma=False,
    )
```

```python
import functools
import math

import jax
import jax.numpy as jnp
import numpy as np
from jax import lax
from jax.experimental import pallas as pl
from jax.experimental.pallas import tpu as pltpu
from jax.sharding import PartitionSpec as P

MODEL_WIDTH = 5120
HEAD_SIZE = 128
BLOCK = 128
LISTED = 10
NBLK = 6
GROUPS = 16
NB = 96
RANK = 64
HEADS = 3
SHARD = 640
TIME_PAIRS = 22
SPACE_PAIRS = 42
N_HEAD = 8
MESH = pl.DeviceIdType.MESH
F32 = jnp.float32
BF16 = jnp.bfloat16

OFFSETS = ((1, 0, 4), (-1, 4, 4), (2, 8, 2), (-2, 10, 2), (3, 12, 1), (-3, 13, 1), (8, 14, 2))
SLOTS = 16


def rope_constants():
    lanes = np.zeros((8, 128), np.float64)
    t = 10000.0 ** (-np.arange(TIME_PAIRS) / TIME_PAIRS)
    s = 10000.0 ** (-np.arange(SPACE_PAIRS) / SPACE_PAIRS)
    lanes[0] = np.concatenate([t, t, s, s])
    lanes[1] = np.concatenate(
        [-np.ones(TIME_PAIRS), np.ones(TIME_PAIRS), -np.ones(SPACE_PAIRS), np.ones(SPACE_PAIRS)]
    )
    lanes[2, : 2 * TIME_PAIRS] = 1.0
    return lanes.astype(np.float32)


def sin_cos(x):
    turns = jnp.floor(x * (1.0 / (2.0 * math.pi)) + 0.5)
    c1 = 6.28125
    c2 = float(np.float32(np.round((2 * math.pi - c1) * 2**20) / 2**20))
    c3 = 2 * math.pi - c1 - c2
    r = ((x - turns * c1) - turns * c2) - turns * c3
    r2 = r * r
    s = jnp.full_like(r, -1.0 / math.factorial(19))
    for n in (17, 15, 13, 11, 9, 7, 5, 3, 1):
        s = s * r2 + (1.0 if n % 4 == 1 else -1.0) / math.factorial(n)
    c = jnp.full_like(r, 1.0 / math.factorial(20))
    for n in (18, 16, 14, 12, 10, 8, 6, 4, 2, 0):
        c = c * r2 + (1.0 if n % 4 == 0 else -1.0) / math.factorial(n)
    return s * r, c


def kernel(
    tok, tabv, tabs, mbf, consts, wq, dn, up, wo, od, ou,
    out, wog,
    xg, wv, dnv, upv, cosv, sinv, planv, plans, acc, accl, qv, own, sb, pool0, pool1, pool2, sc,
    wov, odl, odg, attg, oacc, lacc,
    loc_sem, ag_send, ag_recv, kv_send, kv_recv, plan_sem,
    wz_send, wz_recv, wr_send, wr_recv, at_send, at_recv,
):
    f = lax.axis_index("frame")
    h = lax.axis_index("head")
    z = h // 2
    core = h % 2
    up_h = ((z + 1) % 4) * 2 + core
    dn_h = ((z + 3) % 4) * 2 + core
    far_h = ((z + 2) % 4) * 2 + core
    other = z * 2 + (1 - core)
    f8 = (f + 8) % GROUPS
    y = f // 4
    x = f % 4
    x_up = y * 4 + (x + 1) % 4
    x_dn = y * 4 + (x + 3) % 4
    y_up = ((y + 1) % 4) * 4 + x
    y_dn = ((y + 3) % 4) * 4 + x
    pools = (pool0, pool1, pool2)

    def target(d):
        if d == 8:
            return f8, None
        dst = f + d
        return dst, (dst >= 0) & (dst < GROUPS)

    rows_all = pl.ds(0, NBLK * BLOCK)
    ld_tok = pltpu.make_async_copy(
        tok, xg.at[rows_all, pl.ds(pl.multiple_of(h * SHARD, 128), SHARD)], loc_sem.at[0]
    )
    ld_w = pltpu.make_async_copy(wq, wv, loc_sem.at[1])
    ld_dn = pltpu.make_async_copy(dn, dnv, loc_sem.at[2])
    ld_od = [
        pltpu.make_async_copy(od.at[:, a * 128 : (a + 1) * 128], odl.at[a], loc_sem.at[3 + a])
        for a in range(HEADS)
    ]
    ld_tok.start()
    for cp in ld_od:
        cp.start()
    ld_w.start()
    ld_dn.start()

    barrier = pltpu.get_barrier_semaphore()
    for j in range(1, N_HEAD):
        pl.semaphore_signal(barrier, inc=1, device_id=(f, (h + j) % N_HEAD), device_id_type=MESH)
    for ff in (x_up, x_dn, y_up, y_dn):
        pl.semaphore_signal(barrier, inc=1, device_id=(ff, h), device_id_type=MESH)
    for d, _, _ in OFFSETS:
        dst, ok = target(d)

        def greet(dst=dst):
            pl.semaphore_signal(barrier, inc=1, device_id=(dst, h), device_id_type=MESH)

        if ok is None:
            greet()
        else:
            pl.when(ok)(greet)
    count = N_HEAD - 1 + 4 + 1
    for d in (1, -1, 2, -2, 3, -3):
        count = count + ((f + d >= 0) & (f + d < GROUPS)).astype(jnp.int32)
    pl.semaphore_wait(barrier, count)

    def cols(hh):
        return pl.ds(pl.multiple_of(hh * SHARD, 128), SHARD)

    def rows(r, start=0, size=BLOCK):
        return pl.ds(pl.multiple_of(r * BLOCK + start, 64), size)

    def ag_copy(kind, r, src_h, dst_h, start=0, size=BLOCK, from_tok=False):
        dst = xg.at[rows(r, start, size), cols(src_h)]
        src = tok.at[rows(r, start, size), :] if from_tok else dst
        return pltpu.make_async_remote_copy(
            src_ref=src, dst_ref=dst, send_sem=ag_send.at[kind, r], recv_sem=ag_recv.at[kind, r],
            device_id=(f, dst_h), device_id_type=MESH,
        )

    def wz_copy(j):
        dst_h = (h + j) % N_HEAD
        mine = jnp.where(h < 4, 4 * y + x, 4 * x + y)
        part = pl.ds(pl.multiple_of(mine * 8, 8), 8)
        src = wo.at[:, part, pl.ds(pl.multiple_of(dst_h * SHARD, 128), SHARD)]
        dst = wog.at[:, h, part, :]
        if j == 0:
            return pltpu.make_async_copy(src, dst, wz_send.at[0])
        return pltpu.make_async_remote_copy(
            src_ref=src, dst_ref=dst, send_sem=wz_send.at[j], recv_sem=wz_recv.at[j],
            device_id=(f, dst_h), device_id_type=MESH,
        )

    def ring_copy(half, stage, kind):
        along_x = half == stage
        here = x if along_x else y
        fixed = y if along_x else x
        if stage == 0:
            size = 8
            at = fixed * 4 + (here + 3) % 4 if kind == 2 else fixed * 4 + (here + 1) % 4 if kind == 3 else fixed * 4 + here
        else:
            size = 32
            at = (here + 3) % 4 if kind == 2 else (here + 1) % 4 if kind == 3 else here
        part = pl.ds(pl.multiple_of(at * size, 8), size)
        lo = 4 * half + (2 if kind == 3 else 0)
        n = 4 if kind < 2 else 2
        ref = wog.at[:, lo : lo + n, part, :]
        plus = kind in (0, 2)
        dst = (x_up if plus else x_dn) if along_x else (y_up if plus else y_dn)
        return pltpu.make_async_remote_copy(
            src_ref=ref, dst_ref=ref, send_sem=wr_send.at[half * 2 + stage, kind],
            recv_sem=wr_recv.at[half * 2 + stage, kind],
            device_id=(dst, h), device_id_type=MESH,
        )

    def weights_step(i):
        if i == 0:
            wz_copy(0).wait()
            for j in range(1, N_HEAD):
                wz_copy(j).wait_recv()
            for half in range(2):
                ring_copy(half, 0, 0).start()
                ring_copy(half, 0, 1).start()
        elif i == 1 or i == 3:
            for half in range(2):
                for kind in range(2):
                    ring_copy(half, i // 2, kind).wait_recv()
                    ring_copy(half, i // 2, kind + 2).start()
        else:
            for half in range(2):
                for kind in range(2, 4):
                    ring_copy(half, i // 2 - 1, kind).wait_recv()
            if i == 2:
                for half in range(2):
                    ring_copy(half, 1, 0).start()
                    ring_copy(half, 1, 1).start()

    def lanes(hh):
        return pl.ds(pl.multiple_of(hh * 128, 128), 128)

    def column_ring(view, i, src=None):
        def cp(kind, src_h, dst_h, half=None):
            dst = view(src_h, half)
            return pltpu.make_async_remote_copy(
                src_ref=src if src is not None and kind < 3 else dst, dst_ref=dst,
                send_sem=at_send.at[kind, i], recv_sem=at_recv.at[kind, i],
                device_id=(f, dst_h), device_id_type=MESH,
            )

        return (
            cp(0, h, up_h), cp(1, h, dn_h), cp(2, h, other),
            cp(3, dn_h, up_h, 0), cp(4, up_h, dn_h, 1),
            cp(5, dn_h, other), cp(6, up_h, other),
            cp(7, far_h, other, 0), cp(8, far_h, other, 1),
        )

    def advance(ring):
        ring[0].wait_recv()
        ring[3].start()
        ring[5].start()
        ring[1].wait_recv()
        ring[4].start()
        ring[6].start()

    def spread(ring):
        ring[3].wait_recv()
        ring[7].start()
        ring[4].wait_recv()
        ring[8].start()

    def settle(ring):
        for i in (2, 5, 6, 7, 8):
            ring[i].wait_recv()

    HALF = BLOCK // 2
    def own_up(r):
        return ag_copy(0, r, h, up_h, from_tok=True)

    def own_dn(r):
        return ag_copy(1, r, h, dn_h, from_tok=True)

    def own_other(r):
        return ag_copy(2, r, h, other, from_tok=True)

    def relay_up(r):
        return ag_copy(3, r, dn_h, up_h, 0, HALF)

    def relay_dn(r):
        return ag_copy(4, r, up_h, dn_h, HALF, HALF)

    def share_dn(r):
        return ag_copy(5, r, dn_h, other)

    def share_up(r):
        return ag_copy(6, r, up_h, other)

    def share_far0(r):
        return ag_copy(7, r, far_h, other, 0, HALF)

    def share_far1(r):
        return ag_copy(8, r, far_h, other, HALF, HALF)

    def start_own(r):
        own_up(r).start()
        own_dn(r).start()
        own_other(r).start()

    for j in range(N_HEAD):
        wz_copy(j).start()
    start_own(0)
    start_own(1)

    tab = tabv[...]
    gi = lax.broadcasted_iota(jnp.int32, (NB, NB), 0)
    ri = lax.broadcasted_iota(jnp.int32, (NB, NB), 1)
    member = jnp.zeros((NB, NB), F32)
    for k in range(LISTED):
        member = jnp.maximum(member, (jnp.broadcast_to(tab[k : k + 1, :], (NB, NB)) == gi).astype(F32))
    rq = lax.broadcasted_iota(jnp.int32, (NB, 128), 0)
    qq = lax.broadcasted_iota(jnp.int32, (NB, 128), 1)
    in_group = ((rq * 43) >> 8 == qq).astype(F32)
    used = (jnp.dot(member, in_group, preferred_element_type=F32) > 0.5).astype(F32)
    lower = (((gi * 43) >> 8 == (ri * 43) >> 8) & (ri < gi)).astype(F32)
    rank = jnp.dot(lower, used, preferred_element_type=F32)
    code = jnp.where(used > 0.5, rank, -1.0)
    mine = jnp.sum(jnp.where(qq == f, rank, 0.0), axis=1, keepdims=True)
    delta = ((rq * 43) >> 8) - f
    base = jnp.zeros((NB, 128), F32)
    for d, slot, _ in OFFSETS:
        hit = (delta == -d) if d != 8 else ((delta == 8) | (delta == -8))
        base = jnp.where(hit, float(NBLK + slot), base)
    place = jnp.where(delta == 0, (rq - NBLK * f).astype(F32), base + mine)
    planv[...] = jnp.where(qq == 127, place, code).astype(jnp.int32)
    plan_cp = pltpu.make_async_copy(planv, plans, plan_sem)
    plan_cp.start()

    freq = consts[0:1, :]
    sign = consts[1:2, :]
    timed = consts[2:3, :] > 0.5
    inner = lax.broadcasted_iota(jnp.int32, (BLOCK, 128), 0)

    def table(b, carry):
        g = f * NBLK + b
        fr = mbf[g]

        def tally(i, n):
            return n + (mbf[i] < fr).astype(jnp.int32)

        first = lax.fori_loop(0, NB, tally, jnp.int32(0))
        pos = ((g - first) * BLOCK + inner).astype(F32)
        frame_pos = jnp.zeros((BLOCK, 128), F32) + fr.astype(F32)
        angle = jnp.where(jnp.broadcast_to(timed, (BLOCK, 128)), frame_pos, pos) * freq
        sn, cs = sin_cos(angle)
        cosv[rows(b), :] = cs
        sinv[rows(b), :] = sn * sign
        return carry

    lax.fori_loop(0, NBLK, table, 0)

    upv[...] = jnp.zeros_like(upv)
    for s in range(3):
        upv[s, s * RANK : (s + 1) * RANK, :] = up[s]

    weights_step(0)
    ld_tok.wait()
    ld_w.wait()
    ld_dn.wait()
    plan_cp.wait()

    lane = lax.broadcasted_iota(jnp.int32, (BLOCK, 128), 1)

    def rope(u, cs, sn):
        rot = jnp.where(
            lane < TIME_PAIRS,
            pltpu.roll(u, 128 - TIME_PAIRS, 1),
            jnp.where(
                lane < 2 * TIME_PAIRS,
                pltpu.roll(u, TIME_PAIRS, 1),
                jnp.where(
                    lane < 2 * TIME_PAIRS + SPACE_PAIRS,
                    pltpu.roll(u, 128 - SPACE_PAIRS, 1),
                    pltpu.roll(u, SPACE_PAIRS, 1),
                ),
            ),
        )
        return u * cs + rot * sn

    KC = 1280

    def compute(r):
        def step(k, carry):
            ks = pl.ds(pl.multiple_of(k * KC, 128), KC)
            xk = xg[rows(r), ks]
            keep = (k > 0).astype(F32)
            for s in range(3):
                part = jnp.dot(xk, wv[s, ks, :], preferred_element_type=F32)
                acc[s] = jnp.where(k > 0, acc[s], 0.0) + part
            low = lax.dot_general(xk, dnv[:, ks], (((1,), (1,)), ((), ())), preferred_element_type=F32)
            accl[...] = jnp.where(k > 0, accl[...], 0.0) + low
            return carry

        lax.fori_loop(0, MODEL_WIDTH // KC, step, 0)
        low = accl[...].astype(BF16)
        cs = cosv[rows(r), :]
        sn = sinv[rows(r), :]
        for s in range(3):
            y = acc[s] + jnp.dot(low, upv[s], preferred_element_type=F32)
            for a in range(HEADS):
                u = y[:, a * 128 : (a + 1) * 128]
                if s == 0:
                    qv[a, rows(r), :] = rope(u, cs, sn).astype(BF16)
                elif s == 1:
                    k = rope(u, cs, sn).astype(BF16)
                    own[a, r, 0] = k
                    pools[a][r, 0] = k
                else:
                    v = u.astype(BF16)
                    own[a, r, 1] = v
                    pools[a][r, 1] = v

    def kv_copy(a, slot, dst):
        return pltpu.make_async_remote_copy(
            src_ref=sb.at[a, slot], dst_ref=pools[a].at[NBLK + slot],
            send_sem=kv_send.at[a, slot], recv_sem=kv_recv.at[a, slot],
            device_id=(dst, h), device_id_type=MESH,
        )

    def send_slots(slots):
        picks = []
        for d, slot, rank_of in slots:
            dst, ok = target(d)
            col = dst if ok is None else jnp.clip(dst, 0, GROUPS - 1)
            idx = jnp.int32(0)
            for b in range(1, NBLK):
                idx = jnp.where(plans[f * NBLK + b, col] == rank_of, b, idx)
            picks.append((dst, ok, slot, idx))
        for a in range(HEADS):
            for dst, ok, slot, idx in picks:

                def go(dst=dst, slot=slot, idx=idx, a=a):
                    sb[a, slot] = own[a, idx]
                    kv_copy(a, slot, dst).start()

                if ok is None:
                    go()
                else:
                    pl.when(ok)(go)

    def finish(r):
        relay_up(r).wait_recv()
        share_far0(r).start()
        relay_dn(r).wait_recv()
        share_far1(r).start()
        own_other(r).wait_recv()
        share_dn(r).wait_recv()
        share_up(r).wait_recv()
        share_far0(r).wait_recv()
        share_far1(r).wait_recv()
        compute(r)
        for ready in range(NBLK):
            slots = [
                (d, first + i, i)
                for d, first, n in OFFSETS
                for i in range(n)
                if NBLK - n + i == ready
            ]
            if slots:

                @pl.when(r == ready)
                def _():
                    send_slots(slots)

    def ring(r, carry):
        own_up(r).wait_recv()
        relay_up(r).start()
        share_dn(r).start()
        own_dn(r).wait_recv()
        relay_dn(r).start()
        share_up(r).start()

        @pl.when(r + 2 < NBLK)
        def _():
            start_own(r + 2)

        for i, at in ((1, 1), (2, 2), (3, 4)):

            @pl.when(r == at)
            def _():
                weights_step(i)

        @pl.when(r > 0)
        def _():
            finish(r - 1)

        return carry

    lax.fori_loop(0, NBLK, ring, 0)
    od_ring = column_ring(
        lambda hh, half: odg.at[:, slice(0, RANK) if half is None else slice(32 * half, 32 * half + 32), lanes(hh)],
        NBLK, odl,
    )
    for cp in ld_od:
        cp.wait()
    for a in range(HEADS):
        odg[a, :, lanes(h)] = odl[a]
    for i in range(3):
        od_ring[i].start()
    finish(NBLK - 1)
    advance(od_ring)
    spread(od_ring)
    settle(od_ring)

    def drain(r, carry):
        for cp in (own_up, own_dn, own_other, relay_up, relay_dn, share_dn, share_up, share_far0, share_far1):
            cp(r).wait_send()
        return carry

    scale = math.log2(math.e) / math.sqrt(HEAD_SIZE)

    def attend(a, b, carry):
        pool = pools[a]
        q = qv[a, rows(b), :]
        idx = [
            jnp.clip(plans[tabs[k, f * NBLK + b], 127], 0, NBLK + SLOTS - 1) for k in range(LISTED)
        ]
        top = None
        for k in range(0, LISTED, 2):
            kk = jnp.concatenate([pool[idx[k], 0], pool[idx[k + 1], 0]], axis=0)
            s = lax.dot_general(q, kk, (((1,), (1,)), ((), ())), preferred_element_type=F32)
            sc[:, k * 128 : (k + 2) * 128] = s
            part = jnp.maximum(s[:, :128], s[:, 128:])
            top = part if top is None else jnp.maximum(top, part)
        m = jnp.max(top, axis=1, keepdims=True)
        total = None
        o = None
        for k in range(0, LISTED, 2):
            p = jnp.exp2((sc[:, k * 128 : (k + 2) * 128] - m) * scale)
            t = p[:, :128] + p[:, 128:]
            total = t if total is None else total + t
            vv = jnp.concatenate([pool[idx[k], 1], pool[idx[k + 1], 1]], axis=0)
            po = jnp.dot(p.astype(BF16), vv, preferred_element_type=F32)
            o = po if o is None else o + po
        l = jnp.sum(total, axis=1, keepdims=True)
        attg[a, rows(b), lanes(h)] = (o / l).astype(BF16)
        return carry

    PART = 3 * BLOCK

    def at_ring(i):
        a, c = i // 2, i % 2

        def view(hh, half):
            start = c * PART + (0 if half is None else half * (PART // 2))
            return attg.at[a, start : start + (PART if half is None else PART // 2), lanes(hh)]

        return column_ring(view, i)

    def project(i):
        a, c = i // 2, i % 2

        def go(b, carry):
            xa = attg[a, rows(b), :]
            part = jnp.dot(xa, wov[a].reshape(N_HEAD * 128, SHARD), preferred_element_type=F32)
            low = lax.dot_general(xa, odg[a], (((1,), (1,)), ((), ())), preferred_element_type=F32)
            if a == 0:
                oacc[rows(b), :] = part
                lacc[rows(b), :] = low
            elif a == 1:
                oacc[rows(b), :] += part
                lacc[rows(b), :] += low
            else:
                low = (lacc[rows(b), :] + low).astype(BF16)
                total = oacc[rows(b), :] + part
                out[rows(b), :] = (
                    total + jnp.dot(low, ou[...], preferred_element_type=F32)
                ).astype(BF16)
            return carry

        lax.fori_loop(c * 3, c * 3 + 3, go, 0)

    ld_wo = pltpu.make_async_copy(wog, wov, loc_sem.at[6])
    rings = [at_ring(i) for i in range(2 * HEADS)]
    for i in range(2 * HEADS):
        a, c = i // 2, i % 2
        if c == 0:
            for d, first, n in OFFSETS:
                src = f8 if d == 8 else f - d

                def arrive(first=first, n=n, a=a):
                    for j in range(n):
                        kv_copy(a, first + j, f8).wait_recv()

                if d == 8:
                    arrive()
                else:
                    pl.when((src >= 0) & (src < GROUPS))(arrive)
        lax.fori_loop(c * 3, c * 3 + 3, functools.partial(attend, a), 0)
        for j in range(3):
            rings[i][j].start()
        if i == 0:
            weights_step(4)
            ld_wo.start()
        if i >= 1:
            advance(rings[i - 1])
        if i >= 2:
            spread(rings[i - 2])
        if i == 3:
            ld_wo.wait()
        if i >= 3:
            settle(rings[i - 3])
            project(i - 3)
    advance(rings[5])
    spread(rings[4])
    settle(rings[3])
    project(3)
    spread(rings[5])
    settle(rings[4])
    project(4)
    settle(rings[5])
    project(5)

    for ring in rings + [od_ring]:
        for cp in ring:
            cp.wait_send()
    for j in range(1, N_HEAD):
        wz_copy(j).wait_send()
    for half in range(2):
        for stage in range(2):
            for kind in range(4):
                ring_copy(half, stage, kind).wait_send()
    lax.fori_loop(0, NBLK, drain, 0)
    for a in range(HEADS):
        for d, first, n in OFFSETS:
            dst, ok = target(d)

            def sent(first=first, n=n, a=a, dst=dst):
                for i in range(n):
                    kv_copy(a, first + i, f8).wait_send()

            if ok is None:
                sent()
            else:
                pl.when(ok)(sent)


def body(
    tokens,
    mask_block_frame,
    attended_key_blocks,
    frozen_query_key_value,
    query_key_value_down_weight,
    query_key_value_up_weight,
    frozen_output_weight,
    output_down_weight,
    output_up_weight,
):
    rows = tokens.shape[0]
    width = frozen_output_weight.shape[0]
    table = attended_key_blocks.T
    any_spec = pl.BlockSpec(memory_space=pl.ANY)
    vmem = pl.BlockSpec(memory_space=pltpu.VMEM)
    smem = pl.BlockSpec(memory_space=pltpu.SMEM)
    out, _ = pl.pallas_call(
        kernel,
        out_shape=(
            jax.ShapeDtypeStruct((rows, SHARD), BF16),
            jax.ShapeDtypeStruct((HEADS, N_HEAD, 128, SHARD), BF16),
        ),
        in_specs=[
            any_spec, vmem, smem, smem, vmem, any_spec, any_spec, vmem, any_spec, any_spec, vmem
        ],
        out_specs=(vmem, any_spec),
        scratch_shapes=[
            pltpu.VMEM((rows, MODEL_WIDTH), BF16),
            pltpu.VMEM((3, MODEL_WIDTH, width), BF16),
            pltpu.VMEM((3 * RANK, MODEL_WIDTH), BF16),
            pltpu.VMEM((3, 3 * RANK, width), BF16),
            pltpu.VMEM((rows, 128), F32),
            pltpu.VMEM((rows, 128), F32),
            pltpu.VMEM((NB, 128), jnp.int32),
            pltpu.SMEM((NB, 128), jnp.int32),
            pltpu.VMEM((3, BLOCK, width), F32),
            pltpu.VMEM((BLOCK, 3 * RANK), F32),
            pltpu.VMEM((HEADS, rows, 128), BF16),
            pltpu.VMEM((HEADS, NBLK, 2, BLOCK, 128), BF16),
            pltpu.VMEM((HEADS, SLOTS, 2, BLOCK, 128), BF16),
            pltpu.VMEM((NBLK + SLOTS, 2, BLOCK, 128), BF16),
            pltpu.VMEM((NBLK + SLOTS, 2, BLOCK, 128), BF16),
            pltpu.VMEM((NBLK + SLOTS, 2, BLOCK, 128), BF16),
            pltpu.VMEM((BLOCK, LISTED * BLOCK), F32),
            pltpu.VMEM((HEADS, N_HEAD, 128, SHARD), BF16),
            pltpu.VMEM((HEADS, RANK, 128), BF16),
            pltpu.VMEM((HEADS, RANK, N_HEAD * 128), BF16),
            pltpu.VMEM((HEADS, rows, N_HEAD * 128), BF16),
            pltpu.VMEM((rows, SHARD), F32),
            pltpu.VMEM((rows, RANK), F32),
            pltpu.SemaphoreType.DMA((7,)),
            pltpu.SemaphoreType.DMA((9, NBLK)),
            pltpu.SemaphoreType.DMA((9, NBLK)),
            pltpu.SemaphoreType.DMA((HEADS, SLOTS)),
            pltpu.SemaphoreType.DMA((HEADS, SLOTS)),
            pltpu.SemaphoreType.DMA,
            pltpu.SemaphoreType.DMA((N_HEAD,)),
            pltpu.SemaphoreType.DMA((N_HEAD,)),
            pltpu.SemaphoreType.DMA((4, 4)),
            pltpu.SemaphoreType.DMA((4, 4)),
            pltpu.SemaphoreType.DMA((9, NBLK + 1)),
            pltpu.SemaphoreType.DMA((9, NBLK + 1)),
        ],
        compiler_params=pltpu.CompilerParams(
            collective_id=0, has_side_effects=True, vmem_limit_bytes=62 * 1024 * 1024
        ),
    )(
        tokens,
        table,
        table,
        mask_block_frame,
        jnp.asarray(rope_constants()),
        frozen_query_key_value.transpose(1, 0, 2),
        query_key_value_down_weight.T,
        query_key_value_up_weight.transpose(1, 0, 2),
        frozen_output_weight.reshape(HEADS, 128, MODEL_WIDTH),
        output_down_weight.T,
        output_up_weight,
    )
    return out


def solution(mesh):
    return jax.shard_map(
        body,
        mesh=mesh,
        in_specs=(
            P("frame", "head"),
            P(),
            P(),
            P(None, None, "head"),
            P(),
            P(None, None, "head"),
            P("head", None),
            P("head", None),
            P(None, "head"),
        ),
        out_specs=P("frame", "head"),
        check_vma=False,
    )
```

```python
import functools
import math

import jax
import jax.numpy as jnp
import numpy as np
from jax import lax
from jax.experimental import pallas as pl
from jax.experimental.pallas import tpu as pltpu
from jax.sharding import PartitionSpec as P

MODEL_WIDTH = 5120
HEAD_SIZE = 128
BLOCK = 128
LISTED = 10
NBLK = 6
GROUPS = 16
NB = 96
RANK = 64
HEADS = 3
SHARD = 640
TIME_PAIRS = 22
SPACE_PAIRS = 42
N_HEAD = 8
MESH = pl.DeviceIdType.MESH
F32 = jnp.float32
BF16 = jnp.bfloat16

OFFSETS = ((1, 0, 4), (-1, 4, 4), (2, 8, 2), (-2, 10, 2), (3, 12, 1), (-3, 13, 1), (8, 14, 2))
SLOTS = 16


def rope_constants():
    lanes = np.zeros((8, 128), np.float64)
    t = 10000.0 ** (-np.arange(TIME_PAIRS) / TIME_PAIRS)
    s = 10000.0 ** (-np.arange(SPACE_PAIRS) / SPACE_PAIRS)
    lanes[0] = np.concatenate([t, t, s, s])
    lanes[1] = np.concatenate(
        [-np.ones(TIME_PAIRS), np.ones(TIME_PAIRS), -np.ones(SPACE_PAIRS), np.ones(SPACE_PAIRS)]
    )
    lanes[2, : 2 * TIME_PAIRS] = 1.0
    return lanes.astype(np.float32)


def sin_cos(x):
    turns = jnp.floor(x * (1.0 / (2.0 * math.pi)) + 0.5)
    c1 = 6.28125
    c2 = float(np.float32(np.round((2 * math.pi - c1) * 2**20) / 2**20))
    c3 = 2 * math.pi - c1 - c2
    r = ((x - turns * c1) - turns * c2) - turns * c3
    r2 = r * r
    s = jnp.full_like(r, -1.0 / math.factorial(19))
    for n in (17, 15, 13, 11, 9, 7, 5, 3, 1):
        s = s * r2 + (1.0 if n % 4 == 1 else -1.0) / math.factorial(n)
    c = jnp.full_like(r, 1.0 / math.factorial(20))
    for n in (18, 16, 14, 12, 10, 8, 6, 4, 2, 0):
        c = c * r2 + (1.0 if n % 4 == 0 else -1.0) / math.factorial(n)
    return s * r, c


def kernel(
    tok, tabv, tabs, mbf, consts, wq, dn, up, wo, od, ou,
    out, wog,
    xg, wv, dnv, upv, cosv, sinv, planv, plans, acc, accl, qv, own, sb, pool0, pool1, pool2, sc,
    wov, odl, odg, attg, oacc, lacc,
    loc_sem, ag_send, ag_recv, kv_send, kv_recv, plan_sem,
    wz_send, wz_recv, wr_send, wr_recv, at_send, at_recv,
):
    f = lax.axis_index("frame")
    h = lax.axis_index("head")
    z = h // 2
    core = h % 2
    up_h = ((z + 1) % 4) * 2 + core
    dn_h = ((z + 3) % 4) * 2 + core
    far_h = ((z + 2) % 4) * 2 + core
    other = z * 2 + (1 - core)
    f8 = (f + 8) % GROUPS
    y = f // 4
    x = f % 4
    x_up = y * 4 + (x + 1) % 4
    x_dn = y * 4 + (x + 3) % 4
    y_up = ((y + 1) % 4) * 4 + x
    y_dn = ((y + 3) % 4) * 4 + x
    pools = (pool0, pool1, pool2)

    def target(d):
        if d == 8:
            return f8, None
        dst = f + d
        return dst, (dst >= 0) & (dst < GROUPS)

    rows_all = pl.ds(0, NBLK * BLOCK)
    ld_tok = pltpu.make_async_copy(
        tok, xg.at[rows_all, pl.ds(pl.multiple_of(h * SHARD, 128), SHARD)], loc_sem.at[0]
    )
    ld_w = pltpu.make_async_copy(wq, wv, loc_sem.at[1])
    ld_dn = pltpu.make_async_copy(dn, dnv, loc_sem.at[2])
    ld_od = [
        pltpu.make_async_copy(od.at[:, a * 128 : (a + 1) * 128], odl.at[a], loc_sem.at[3 + a])
        for a in range(HEADS)
    ]
    ld_tok.start()
    for cp in ld_od:
        cp.start()
    ld_w.start()
    ld_dn.start()

    barrier = pltpu.get_barrier_semaphore()
    for j in range(1, N_HEAD):
        pl.semaphore_signal(barrier, inc=1, device_id=(f, (h + j) % N_HEAD), device_id_type=MESH)
    for ff in (x_up, x_dn, y_up, y_dn):
        pl.semaphore_signal(barrier, inc=1, device_id=(ff, h), device_id_type=MESH)
    for d, _, _ in OFFSETS:
        dst, ok = target(d)

        def greet(dst=dst):
            pl.semaphore_signal(barrier, inc=1, device_id=(dst, h), device_id_type=MESH)

        if ok is None:
            greet()
        else:
            pl.when(ok)(greet)
    count = N_HEAD - 1 + 4 + 1
    for d in (1, -1, 2, -2, 3, -3):
        count = count + ((f + d >= 0) & (f + d < GROUPS)).astype(jnp.int32)
    pl.semaphore_wait(barrier, count)

    def cols(hh):
        return pl.ds(pl.multiple_of(hh * SHARD, 128), SHARD)

    def rows(r, start=0, size=BLOCK):
        return pl.ds(pl.multiple_of(r * BLOCK + start, 64), size)

    def ag_copy(kind, r, src_h, dst_h, start=0, size=BLOCK, from_tok=False):
        dst = xg.at[rows(r, start, size), cols(src_h)]
        src = tok.at[rows(r, start, size), :] if from_tok else dst
        return pltpu.make_async_remote_copy(
            src_ref=src, dst_ref=dst, send_sem=ag_send.at[kind, r], recv_sem=ag_recv.at[kind, r],
            device_id=(f, dst_h), device_id_type=MESH,
        )

    def wz_copy(j):
        dst_h = (h + j) % N_HEAD
        mine = jnp.where(h < 4, 4 * y + x, 4 * x + y)
        part = pl.ds(pl.multiple_of(mine * 8, 8), 8)
        src = wo.at[:, part, pl.ds(pl.multiple_of(dst_h * SHARD, 128), SHARD)]
        dst = wog.at[:, h, part, :]
        if j == 0:
            return pltpu.make_async_copy(src, dst, wz_send.at[0])
        return pltpu.make_async_remote_copy(
            src_ref=src, dst_ref=dst, send_sem=wz_send.at[j], recv_sem=wz_recv.at[j],
            device_id=(f, dst_h), device_id_type=MESH,
        )

    def ring_copy(half, stage, kind):
        along_x = half == stage
        here = x if along_x else y
        fixed = y if along_x else x
        if stage == 0:
            size = 8
            at = fixed * 4 + (here + 3) % 4 if kind == 2 else fixed * 4 + (here + 1) % 4 if kind == 3 else fixed * 4 + here
        else:
            size = 32
            at = (here + 3) % 4 if kind == 2 else (here + 1) % 4 if kind == 3 else here
        part = pl.ds(pl.multiple_of(at * size, 8), size)
        lo = 4 * half + (2 if kind == 3 else 0)
        n = 4 if kind < 2 else 2
        ref = wog.at[:, lo : lo + n, part, :]
        plus = kind in (0, 2)
        dst = (x_up if plus else x_dn) if along_x else (y_up if plus else y_dn)
        return pltpu.make_async_remote_copy(
            src_ref=ref, dst_ref=ref, send_sem=wr_send.at[half * 2 + stage, kind],
            recv_sem=wr_recv.at[half * 2 + stage, kind],
            device_id=(dst, h), device_id_type=MESH,
        )

    def weights_step(i):
        if i == 0:
            wz_copy(0).wait()
            for j in range(1, N_HEAD):
                wz_copy(j).wait_recv()
            for half in range(2):
                ring_copy(half, 0, 0).start()
                ring_copy(half, 0, 1).start()
        elif i == 1 or i == 3:
            for half in range(2):
                for kind in range(2):
                    ring_copy(half, i // 2, kind).wait_recv()
                    ring_copy(half, i // 2, kind + 2).start()
        else:
            for half in range(2):
                for kind in range(2, 4):
                    ring_copy(half, i // 2 - 1, kind).wait_recv()
            if i == 2:
                for half in range(2):
                    ring_copy(half, 1, 0).start()
                    ring_copy(half, 1, 1).start()

    def lanes(hh):
        return pl.ds(pl.multiple_of(hh * 128, 128), 128)

    def column_ring(view, i, src=None):
        def cp(kind, src_h, dst_h, half=None):
            dst = view(src_h, half)
            return pltpu.make_async_remote_copy(
                src_ref=src if src is not None and kind < 3 else dst, dst_ref=dst,
                send_sem=at_send.at[kind, i], recv_sem=at_recv.at[kind, i],
                device_id=(f, dst_h), device_id_type=MESH,
            )

        return (
            cp(0, h, up_h), cp(1, h, dn_h), cp(2, h, other),
            cp(3, dn_h, up_h, 0), cp(4, up_h, dn_h, 1),
            cp(5, dn_h, other), cp(6, up_h, other),
            cp(7, far_h, other, 0), cp(8, far_h, other, 1),
        )

    def advance(ring):
        ring[0].wait_recv()
        ring[3].start()
        ring[5].start()
        ring[1].wait_recv()
        ring[4].start()
        ring[6].start()

    def spread(ring):
        ring[3].wait_recv()
        ring[7].start()
        ring[4].wait_recv()
        ring[8].start()

    def settle(ring):
        for i in (2, 5, 6, 7, 8):
            ring[i].wait_recv()

    HALF = BLOCK // 2
    def own_up(r):
        return ag_copy(0, r, h, up_h, from_tok=True)

    def own_dn(r):
        return ag_copy(1, r, h, dn_h, from_tok=True)

    def own_other(r):
        return ag_copy(2, r, h, other, from_tok=True)

    def relay_up(r):
        return ag_copy(3, r, dn_h, up_h, 0, HALF)

    def relay_dn(r):
        return ag_copy(4, r, up_h, dn_h, HALF, HALF)

    def share_dn(r):
        return ag_copy(5, r, dn_h, other)

    def share_up(r):
        return ag_copy(6, r, up_h, other)

    def share_far0(r):
        return ag_copy(7, r, far_h, other, 0, HALF)

    def share_far1(r):
        return ag_copy(8, r, far_h, other, HALF, HALF)

    def start_own(r):
        own_up(r).start()
        own_dn(r).start()
        own_other(r).start()

    for j in range(N_HEAD):
        wz_copy(j).start()
    start_own(0)
    start_own(1)

    tab = tabv[...]
    gi = lax.broadcasted_iota(jnp.int32, (NB, NB), 0)
    ri = lax.broadcasted_iota(jnp.int32, (NB, NB), 1)
    member = jnp.zeros((NB, NB), F32)
    for k in range(LISTED):
        member = jnp.maximum(member, (jnp.broadcast_to(tab[k : k + 1, :], (NB, NB)) == gi).astype(F32))
    rq = lax.broadcasted_iota(jnp.int32, (NB, 128), 0)
    qq = lax.broadcasted_iota(jnp.int32, (NB, 128), 1)
    in_group = ((rq * 43) >> 8 == qq).astype(F32)
    used = (jnp.dot(member, in_group, preferred_element_type=F32) > 0.5).astype(F32)
    lower = (((gi * 43) >> 8 == (ri * 43) >> 8) & (ri < gi)).astype(F32)
    rank = jnp.dot(lower, used, preferred_element_type=F32)
    code = jnp.where(used > 0.5, rank, -1.0)
    mine = jnp.sum(jnp.where(qq == f, rank, 0.0), axis=1, keepdims=True)
    delta = ((rq * 43) >> 8) - f
    base = jnp.zeros((NB, 128), F32)
    for d, slot, _ in OFFSETS:
        hit = (delta == -d) if d != 8 else ((delta == 8) | (delta == -8))
        base = jnp.where(hit, float(NBLK + slot), base)
    place = jnp.where(delta == 0, (rq - NBLK * f).astype(F32), base + mine)
    planv[...] = jnp.where(qq == 127, place, code).astype(jnp.int32)
    plan_cp = pltpu.make_async_copy(planv, plans, plan_sem)
    plan_cp.start()

    freq = consts[0:1, :]
    sign = consts[1:2, :]
    timed = consts[2:3, :] > 0.5
    inner = lax.broadcasted_iota(jnp.int32, (BLOCK, 128), 0)

    def table(b, carry):
        g = f * NBLK + b
        fr = mbf[g]

        def tally(i, n):
            return n + (mbf[i] < fr).astype(jnp.int32)

        first = lax.fori_loop(0, NB, tally, jnp.int32(0))
        pos = ((g - first) * BLOCK + inner).astype(F32)
        frame_pos = jnp.zeros((BLOCK, 128), F32) + fr.astype(F32)
        angle = jnp.where(jnp.broadcast_to(timed, (BLOCK, 128)), frame_pos, pos) * freq
        sn, cs = sin_cos(angle)
        cosv[rows(b), :] = cs
        sinv[rows(b), :] = sn * sign
        return carry

    lax.fori_loop(0, NBLK, table, 0)

    upv[...] = jnp.zeros_like(upv)
    for s in range(3):
        upv[s, s * RANK : (s + 1) * RANK, :] = up[s]

    weights_step(0)
    ld_tok.wait()
    ld_w.wait()
    ld_dn.wait()
    plan_cp.wait()

    lane = lax.broadcasted_iota(jnp.int32, (BLOCK, 128), 1)

    def rope(u, cs, sn):
        rot = jnp.where(
            lane < TIME_PAIRS,
            pltpu.roll(u, 128 - TIME_PAIRS, 1),
            jnp.where(
                lane < 2 * TIME_PAIRS,
                pltpu.roll(u, TIME_PAIRS, 1),
                jnp.where(
                    lane < 2 * TIME_PAIRS + SPACE_PAIRS,
                    pltpu.roll(u, 128 - SPACE_PAIRS, 1),
                    pltpu.roll(u, SPACE_PAIRS, 1),
                ),
            ),
        )
        return u * cs + rot * sn

    KC = 1280

    def compute(r):
        def step(k, carry):
            ks = pl.ds(pl.multiple_of(k * KC, 128), KC)
            xk = xg[rows(r), ks]
            keep = (k > 0).astype(F32)
            for s in range(3):
                part = jnp.dot(xk, wv[s, ks, :], preferred_element_type=F32)
                acc[s] = jnp.where(k > 0, acc[s], 0.0) + part
            low = lax.dot_general(xk, dnv[:, ks], (((1,), (1,)), ((), ())), preferred_element_type=F32)
            accl[...] = jnp.where(k > 0, accl[...], 0.0) + low
            return carry

        lax.fori_loop(0, MODEL_WIDTH // KC, step, 0)
        low = accl[...].astype(BF16)
        cs = cosv[rows(r), :]
        sn = sinv[rows(r), :]
        for s in range(3):
            y = acc[s] + jnp.dot(low, upv[s], preferred_element_type=F32)
            for a in range(HEADS):
                u = y[:, a * 128 : (a + 1) * 128]
                if s == 0:
                    qv[a, rows(r), :] = rope(u, cs, sn).astype(BF16)
                elif s == 1:
                    k = rope(u, cs, sn).astype(BF16)
                    own[a, r, 0] = k
                    pools[a][r, 0] = k
                else:
                    v = u.astype(BF16)
                    own[a, r, 1] = v
                    pools[a][r, 1] = v

    def kv_copy(a, slot, dst):
        return pltpu.make_async_remote_copy(
            src_ref=sb.at[a, slot], dst_ref=pools[a].at[NBLK + slot],
            send_sem=kv_send.at[a, slot], recv_sem=kv_recv.at[a, slot],
            device_id=(dst, h), device_id_type=MESH,
        )

    def send_slots(slots):
        picks = []
        for d, slot, rank_of in slots:
            dst, ok = target(d)
            col = dst if ok is None else jnp.clip(dst, 0, GROUPS - 1)
            idx = jnp.int32(0)
            for b in range(1, NBLK):
                idx = jnp.where(plans[f * NBLK + b, col] == rank_of, b, idx)
            picks.append((dst, ok, slot, idx))
        for a in range(HEADS):
            for dst, ok, slot, idx in picks:

                def go(dst=dst, slot=slot, idx=idx, a=a):
                    sb[a, slot] = own[a, idx]
                    kv_copy(a, slot, dst).start()

                if ok is None:
                    go()
                else:
                    pl.when(ok)(go)

    def finish(r):
        relay_up(r).wait_recv()
        share_far0(r).start()
        relay_dn(r).wait_recv()
        share_far1(r).start()
        own_other(r).wait_recv()
        share_dn(r).wait_recv()
        share_up(r).wait_recv()
        share_far0(r).wait_recv()
        share_far1(r).wait_recv()
        compute(r)
        for ready in range(NBLK):
            slots = [
                (d, first + i, i)
                for d, first, n in OFFSETS
                for i in range(n)
                if NBLK - n + i == ready
            ]
            if slots:

                @pl.when(r == ready)
                def _():
                    send_slots(slots)

    def ring(r, carry):
        own_up(r).wait_recv()
        relay_up(r).start()
        share_dn(r).start()
        own_dn(r).wait_recv()
        relay_dn(r).start()
        share_up(r).start()

        @pl.when(r + 2 < NBLK)
        def _():
            start_own(r + 2)

        for i, at in ((1, 0), (2, 1), (3, 3)):

            @pl.when(r == at)
            def _():
                weights_step(i)

        @pl.when(r > 0)
        def _():
            finish(r - 1)

        return carry

    lax.fori_loop(0, NBLK, ring, 0)
    od_ring = column_ring(
        lambda hh, half: odg.at[:, slice(0, RANK) if half is None else slice(32 * half, 32 * half + 32), lanes(hh)],
        NBLK, odl,
    )
    for cp in ld_od:
        cp.wait()
    for a in range(HEADS):
        odg[a, :, lanes(h)] = odl[a]
    for i in range(3):
        od_ring[i].start()
    finish(NBLK - 1)
    advance(od_ring)
    spread(od_ring)
    settle(od_ring)

    def drain(r, carry):
        for cp in (own_up, own_dn, own_other, relay_up, relay_dn, share_dn, share_up, share_far0, share_far1):
            cp(r).wait_send()
        return carry

    scale = math.log2(math.e) / math.sqrt(HEAD_SIZE)

    def attend(a, b, carry):
        pool = pools[a]
        q = qv[a, rows(b), :]
        idx = [
            jnp.clip(plans[tabs[k, f * NBLK + b], 127], 0, NBLK + SLOTS - 1) for k in range(LISTED)
        ]
        top = None
        for k in range(0, LISTED, 2):
            kk = jnp.concatenate([pool[idx[k], 0], pool[idx[k + 1], 0]], axis=0)
            s = lax.dot_general(q, kk, (((1,), (1,)), ((), ())), preferred_element_type=F32)
            sc[:, k * 128 : (k + 2) * 128] = s
            part = jnp.maximum(s[:, :128], s[:, 128:])
            top = part if top is None else jnp.maximum(top, part)
        m = jnp.max(top, axis=1, keepdims=True)
        total = None
        o = None
        for k in range(0, LISTED, 2):
            p = jnp.exp2((sc[:, k * 128 : (k + 2) * 128] - m) * scale)
            t = p[:, :128] + p[:, 128:]
            total = t if total is None else total + t
            vv = jnp.concatenate([pool[idx[k], 1], pool[idx[k + 1], 1]], axis=0)
            po = jnp.dot(p.astype(BF16), vv, preferred_element_type=F32)
            o = po if o is None else o + po
        l = jnp.sum(total, axis=1, keepdims=True)
        attg[a, rows(b), lanes(h)] = (o / l).astype(BF16)
        return carry

    PART = 3 * BLOCK

    def at_ring(i):
        a, c = i // 2, i % 2

        def view(hh, half):
            start = c * PART + (0 if half is None else half * (PART // 2))
            return attg.at[a, start : start + (PART if half is None else PART // 2), lanes(hh)]

        return column_ring(view, i)

    def project(i):
        a, c = i // 2, i % 2

        def go(b, carry):
            xa = attg[a, rows(b), :]
            part = jnp.dot(xa, wov[a].reshape(N_HEAD * 128, SHARD), preferred_element_type=F32)
            low = lax.dot_general(xa, odg[a], (((1,), (1,)), ((), ())), preferred_element_type=F32)
            if a == 0:
                oacc[rows(b), :] = part
                lacc[rows(b), :] = low
            elif a == 1:
                oacc[rows(b), :] += part
                lacc[rows(b), :] += low
            else:
                low = (lacc[rows(b), :] + low).astype(BF16)
                total = oacc[rows(b), :] + part
                out[rows(b), :] = (
                    total + jnp.dot(low, ou[...], preferred_element_type=F32)
                ).astype(BF16)
            return carry

        lax.fori_loop(c * 3, c * 3 + 3, go, 0)

    ld_wo = pltpu.make_async_copy(wog, wov, loc_sem.at[6])
    rings = [at_ring(i) for i in range(2 * HEADS)]
    for i in range(2 * HEADS):
        a, c = i // 2, i % 2
        if c == 0:
            for d, first, n in OFFSETS:
                src = f8 if d == 8 else f - d

                def arrive(first=first, n=n, a=a):
                    for j in range(n):
                        kv_copy(a, first + j, f8).wait_recv()

                if d == 8:
                    arrive()
                else:
                    pl.when((src >= 0) & (src < GROUPS))(arrive)
        lax.fori_loop(c * 3, c * 3 + 3, functools.partial(attend, a), 0)
        for j in range(3):
            rings[i][j].start()
        if i == 0:
            weights_step(4)
            ld_wo.start()
        if i >= 1:
            advance(rings[i - 1])
        if i >= 2:
            spread(rings[i - 2])
        if i == 3:
            ld_wo.wait()
        if i >= 3:
            settle(rings[i - 3])
            project(i - 3)
    advance(rings[5])
    spread(rings[4])
    settle(rings[3])
    project(3)
    spread(rings[5])
    settle(rings[4])
    project(4)
    settle(rings[5])
    project(5)

    for ring in rings + [od_ring]:
        for cp in ring:
            cp.wait_send()
    for j in range(1, N_HEAD):
        wz_copy(j).wait_send()
    for half in range(2):
        for stage in range(2):
            for kind in range(4):
                ring_copy(half, stage, kind).wait_send()
    lax.fori_loop(0, NBLK, drain, 0)
    for a in range(HEADS):
        for d, first, n in OFFSETS:
            dst, ok = target(d)

            def sent(first=first, n=n, a=a, dst=dst):
                for i in range(n):
                    kv_copy(a, first + i, f8).wait_send()

            if ok is None:
                sent()
            else:
                pl.when(ok)(sent)


def body(
    tokens,
    mask_block_frame,
    attended_key_blocks,
    frozen_query_key_value,
    query_key_value_down_weight,
    query_key_value_up_weight,
    frozen_output_weight,
    output_down_weight,
    output_up_weight,
):
    rows = tokens.shape[0]
    width = frozen_output_weight.shape[0]
    table = attended_key_blocks.T
    any_spec = pl.BlockSpec(memory_space=pl.ANY)
    vmem = pl.BlockSpec(memory_space=pltpu.VMEM)
    smem = pl.BlockSpec(memory_space=pltpu.SMEM)
    out, _ = pl.pallas_call(
        kernel,
        out_shape=(
            jax.ShapeDtypeStruct((rows, SHARD), BF16),
            jax.ShapeDtypeStruct((HEADS, N_HEAD, 128, SHARD), BF16),
        ),
        in_specs=[
            any_spec, vmem, smem, smem, vmem, any_spec, any_spec, vmem, any_spec, any_spec, vmem
        ],
        out_specs=(vmem, any_spec),
        scratch_shapes=[
            pltpu.VMEM((rows, MODEL_WIDTH), BF16),
            pltpu.VMEM((3, MODEL_WIDTH, width), BF16),
            pltpu.VMEM((3 * RANK, MODEL_WIDTH), BF16),
            pltpu.VMEM((3, 3 * RANK, width), BF16),
            pltpu.VMEM((rows, 128), F32),
            pltpu.VMEM((rows, 128), F32),
            pltpu.VMEM((NB, 128), jnp.int32),
            pltpu.SMEM((NB, 128), jnp.int32),
            pltpu.VMEM((3, BLOCK, width), F32),
            pltpu.VMEM((BLOCK, 3 * RANK), F32),
            pltpu.VMEM((HEADS, rows, 128), BF16),
            pltpu.VMEM((HEADS, NBLK, 2, BLOCK, 128), BF16),
            pltpu.VMEM((HEADS, SLOTS, 2, BLOCK, 128), BF16),
            pltpu.VMEM((NBLK + SLOTS, 2, BLOCK, 128), BF16),
            pltpu.VMEM((NBLK + SLOTS, 2, BLOCK, 128), BF16),
            pltpu.VMEM((NBLK + SLOTS, 2, BLOCK, 128), BF16),
            pltpu.VMEM((BLOCK, LISTED * BLOCK), F32),
            pltpu.VMEM((HEADS, N_HEAD, 128, SHARD), BF16),
            pltpu.VMEM((HEADS, RANK, 128), BF16),
            pltpu.VMEM((HEADS, RANK, N_HEAD * 128), BF16),
            pltpu.VMEM((HEADS, rows, N_HEAD * 128), BF16),
            pltpu.VMEM((rows, SHARD), F32),
            pltpu.VMEM((rows, RANK), F32),
            pltpu.SemaphoreType.DMA((7,)),
            pltpu.SemaphoreType.DMA((9, NBLK)),
            pltpu.SemaphoreType.DMA((9, NBLK)),
            pltpu.SemaphoreType.DMA((HEADS, SLOTS)),
            pltpu.SemaphoreType.DMA((HEADS, SLOTS)),
            pltpu.SemaphoreType.DMA,
            pltpu.SemaphoreType.DMA((N_HEAD,)),
            pltpu.SemaphoreType.DMA((N_HEAD,)),
            pltpu.SemaphoreType.DMA((4, 4)),
            pltpu.SemaphoreType.DMA((4, 4)),
            pltpu.SemaphoreType.DMA((9, NBLK + 1)),
            pltpu.SemaphoreType.DMA((9, NBLK + 1)),
        ],
        compiler_params=pltpu.CompilerParams(
            collective_id=0, has_side_effects=True, vmem_limit_bytes=62 * 1024 * 1024
        ),
    )(
        tokens,
        table,
        table,
        mask_block_frame,
        jnp.asarray(rope_constants()),
        frozen_query_key_value.transpose(1, 0, 2),
        query_key_value_down_weight.T,
        query_key_value_up_weight.transpose(1, 0, 2),
        frozen_output_weight.reshape(HEADS, 128, MODEL_WIDTH),
        output_down_weight.T,
        output_up_weight,
    )
    return out


def solution(mesh):
    return jax.shard_map(
        body,
        mesh=mesh,
        in_specs=(
            P("frame", "head"),
            P(),
            P(),
            P(None, None, "head"),
            P(),
            P(None, None, "head"),
            P("head", None),
            P("head", None),
            P(None, "head"),
        ),
        out_specs=P("frame", "head"),
        check_vma=False,
    )
```

```python
import functools
import math

import jax
import jax.numpy as jnp
import numpy as np
from jax import lax
from jax.experimental import pallas as pl
from jax.experimental.pallas import tpu as pltpu
from jax.sharding import PartitionSpec as P

MODEL_WIDTH = 5120
HEAD_SIZE = 128
BLOCK = 128
LISTED = 10
NBLK = 6
GROUPS = 16
NB = 96
RANK = 64
HEADS = 3
SHARD = 640
TIME_PAIRS = 22
SPACE_PAIRS = 42
N_HEAD = 8
MESH = pl.DeviceIdType.MESH
F32 = jnp.float32
BF16 = jnp.bfloat16

OFFSETS = ((1, 0, 4), (-1, 4, 4), (2, 8, 2), (-2, 10, 2), (3, 12, 1), (-3, 13, 1), (8, 14, 2))
SLOTS = 16


def rope_constants():
    lanes = np.zeros((8, 128), np.float64)
    t = 10000.0 ** (-np.arange(TIME_PAIRS) / TIME_PAIRS)
    s = 10000.0 ** (-np.arange(SPACE_PAIRS) / SPACE_PAIRS)
    lanes[0] = np.concatenate([t, t, s, s])
    lanes[1] = np.concatenate(
        [-np.ones(TIME_PAIRS), np.ones(TIME_PAIRS), -np.ones(SPACE_PAIRS), np.ones(SPACE_PAIRS)]
    )
    lanes[2, : 2 * TIME_PAIRS] = 1.0
    return lanes.astype(np.float32)


def sin_cos(x):
    turns = jnp.floor(x * (1.0 / (2.0 * math.pi)) + 0.5)
    c1 = 6.28125
    c2 = float(np.float32(np.round((2 * math.pi - c1) * 2**20) / 2**20))
    c3 = 2 * math.pi - c1 - c2
    r = ((x - turns * c1) - turns * c2) - turns * c3
    r2 = r * r
    s = jnp.full_like(r, -1.0 / math.factorial(19))
    for n in (17, 15, 13, 11, 9, 7, 5, 3, 1):
        s = s * r2 + (1.0 if n % 4 == 1 else -1.0) / math.factorial(n)
    c = jnp.full_like(r, 1.0 / math.factorial(20))
    for n in (18, 16, 14, 12, 10, 8, 6, 4, 2, 0):
        c = c * r2 + (1.0 if n % 4 == 0 else -1.0) / math.factorial(n)
    return s * r, c


def kernel(
    tok, tabv, tabs, mbf, consts, wq, dn, up, wo, od, ou,
    out, wog,
    xg, wv, dnv, upv, cosv, sinv, planv, plans, acc, accl, qv, own, sb, pool0, pool1, pool2, sc,
    wov, odl, odg, attg, oacc, lacc,
    loc_sem, ag_send, ag_recv, kv_send, kv_recv, plan_sem,
    wz_send, wz_recv, wr_send, wr_recv, at_send, at_recv,
):
    f = lax.axis_index("frame")
    h = lax.axis_index("head")
    z = h // 2
    core = h % 2
    up_h = ((z + 1) % 4) * 2 + core
    dn_h = ((z + 3) % 4) * 2 + core
    far_h = ((z + 2) % 4) * 2 + core
    other = z * 2 + (1 - core)
    f8 = (f + 8) % GROUPS
    y = f // 4
    x = f % 4
    x_up = y * 4 + (x + 1) % 4
    x_dn = y * 4 + (x + 3) % 4
    y_up = ((y + 1) % 4) * 4 + x
    y_dn = ((y + 3) % 4) * 4 + x
    pools = (pool0, pool1, pool2)

    def target(d):
        if d == 8:
            return f8, None
        dst = f + d
        return dst, (dst >= 0) & (dst < GROUPS)

    rows_all = pl.ds(0, NBLK * BLOCK)
    ld_tok = pltpu.make_async_copy(
        tok, xg.at[rows_all, pl.ds(pl.multiple_of(h * SHARD, 128), SHARD)], loc_sem.at[0]
    )
    ld_w = pltpu.make_async_copy(wq, wv, loc_sem.at[1])
    ld_dn = pltpu.make_async_copy(dn, dnv, loc_sem.at[2])
    ld_od = [
        pltpu.make_async_copy(od.at[:, a * 128 : (a + 1) * 128], odl.at[a], loc_sem.at[3 + a])
        for a in range(HEADS)
    ]
    ld_tok.start()
    for cp in ld_od:
        cp.start()
    ld_w.start()
    ld_dn.start()

    barrier = pltpu.get_barrier_semaphore()
    for j in range(1, N_HEAD):
        pl.semaphore_signal(barrier, inc=1, device_id=(f, (h + j) % N_HEAD), device_id_type=MESH)
    for ff in (x_up, x_dn, y_up, y_dn):
        pl.semaphore_signal(barrier, inc=1, device_id=(ff, h), device_id_type=MESH)
    for d, _, _ in OFFSETS:
        dst, ok = target(d)

        def greet(dst=dst):
            pl.semaphore_signal(barrier, inc=1, device_id=(dst, h), device_id_type=MESH)

        if ok is None:
            greet()
        else:
            pl.when(ok)(greet)
    count = N_HEAD - 1 + 4 + 1
    for d in (1, -1, 2, -2, 3, -3):
        count = count + ((f + d >= 0) & (f + d < GROUPS)).astype(jnp.int32)
    pl.semaphore_wait(barrier, count)

    def cols(hh):
        return pl.ds(pl.multiple_of(hh * SHARD, 128), SHARD)

    def rows(r, start=0, size=BLOCK):
        return pl.ds(pl.multiple_of(r * BLOCK + start, 64), size)

    def ag_copy(kind, r, src_h, dst_h, start=0, size=BLOCK, from_tok=False):
        dst = xg.at[rows(r, start, size), cols(src_h)]
        src = tok.at[rows(r, start, size), :] if from_tok else dst
        return pltpu.make_async_remote_copy(
            src_ref=src, dst_ref=dst, send_sem=ag_send.at[kind, r], recv_sem=ag_recv.at[kind, r],
            device_id=(f, dst_h), device_id_type=MESH,
        )

    def wz_copy(j):
        dst_h = (h + j) % N_HEAD
        mine = jnp.where(h < 4, 4 * y + x, 4 * x + y)
        part = pl.ds(pl.multiple_of(mine * 8, 8), 8)
        src = wo.at[:, part, pl.ds(pl.multiple_of(dst_h * SHARD, 128), SHARD)]
        dst = wog.at[:, h, part, :]
        if j == 0:
            return pltpu.make_async_copy(src, dst, wz_send.at[0])
        return pltpu.make_async_remote_copy(
            src_ref=src, dst_ref=dst, send_sem=wz_send.at[j], recv_sem=wz_recv.at[j],
            device_id=(f, dst_h), device_id_type=MESH,
        )

    def ring_copy(half, stage, kind):
        along_x = half == stage
        here = x if along_x else y
        fixed = y if along_x else x
        if stage == 0:
            size = 8
            at = fixed * 4 + (here + 3) % 4 if kind == 2 else fixed * 4 + (here + 1) % 4 if kind == 3 else fixed * 4 + here
        else:
            size = 32
            at = (here + 3) % 4 if kind == 2 else (here + 1) % 4 if kind == 3 else here
        part = pl.ds(pl.multiple_of(at * size, 8), size)
        lo = 4 * half + (2 if kind == 3 else 0)
        n = 4 if kind < 2 else 2
        ref = wog.at[:, lo : lo + n, part, :]
        plus = kind in (0, 2)
        dst = (x_up if plus else x_dn) if along_x else (y_up if plus else y_dn)
        return pltpu.make_async_remote_copy(
            src_ref=ref, dst_ref=ref, send_sem=wr_send.at[half * 2 + stage, kind],
            recv_sem=wr_recv.at[half * 2 + stage, kind],
            device_id=(dst, h), device_id_type=MESH,
        )

    def weights_step(i):
        if i == 0:
            wz_copy(0).wait()
            for j in range(1, N_HEAD):
                wz_copy(j).wait_recv()
            for half in range(2):
                ring_copy(half, 0, 0).start()
                ring_copy(half, 0, 1).start()
        elif i == 1 or i == 3:
            for half in range(2):
                for kind in range(2):
                    ring_copy(half, i // 2, kind).wait_recv()
                    ring_copy(half, i // 2, kind + 2).start()
        else:
            for half in range(2):
                for kind in range(2, 4):
                    ring_copy(half, i // 2 - 1, kind).wait_recv()
            if i == 2:
                for half in range(2):
                    ring_copy(half, 1, 0).start()
                    ring_copy(half, 1, 1).start()

    def lanes(hh):
        return pl.ds(pl.multiple_of(hh * 128, 128), 128)

    def column_ring(view, i, src=None):
        def cp(kind, src_h, dst_h, half=None):
            dst = view(src_h, half)
            return pltpu.make_async_remote_copy(
                src_ref=src if src is not None and kind < 3 else dst, dst_ref=dst,
                send_sem=at_send.at[kind, i], recv_sem=at_recv.at[kind, i],
                device_id=(f, dst_h), device_id_type=MESH,
            )

        return (
            cp(0, h, up_h), cp(1, h, dn_h), cp(2, h, other),
            cp(3, dn_h, up_h, 0), cp(4, up_h, dn_h, 1),
            cp(5, dn_h, other), cp(6, up_h, other),
            cp(7, far_h, other, 0), cp(8, far_h, other, 1),
        )

    def advance(ring):
        ring[0].wait_recv()
        ring[3].start()
        ring[5].start()
        ring[1].wait_recv()
        ring[4].start()
        ring[6].start()

    def spread(ring):
        ring[3].wait_recv()
        ring[7].start()
        ring[4].wait_recv()
        ring[8].start()

    def settle(ring):
        for i in (2, 5, 6, 7, 8):
            ring[i].wait_recv()

    HALF = BLOCK // 2
    def own_up(r):
        return ag_copy(0, r, h, up_h, from_tok=True)

    def own_dn(r):
        return ag_copy(1, r, h, dn_h, from_tok=True)

    def own_other(r):
        return ag_copy(2, r, h, other, from_tok=True)

    def relay_up(r):
        return ag_copy(3, r, dn_h, up_h, 0, HALF)

    def relay_dn(r):
        return ag_copy(4, r, up_h, dn_h, HALF, HALF)

    def share_dn(r):
        return ag_copy(5, r, dn_h, other)

    def share_up(r):
        return ag_copy(6, r, up_h, other)

    def share_far0(r):
        return ag_copy(7, r, far_h, other, 0, HALF)

    def share_far1(r):
        return ag_copy(8, r, far_h, other, HALF, HALF)

    def start_own(r):
        own_up(r).start()
        own_dn(r).start()
        own_other(r).start()

    for j in range(N_HEAD):
        wz_copy(j).start()
    start_own(0)
    start_own(1)

    tab = tabv[...]
    gi = lax.broadcasted_iota(jnp.int32, (NB, NB), 0)
    ri = lax.broadcasted_iota(jnp.int32, (NB, NB), 1)
    member = jnp.zeros((NB, NB), F32)
    for k in range(LISTED):
        member = jnp.maximum(member, (jnp.broadcast_to(tab[k : k + 1, :], (NB, NB)) == gi).astype(F32))
    rq = lax.broadcasted_iota(jnp.int32, (NB, 128), 0)
    qq = lax.broadcasted_iota(jnp.int32, (NB, 128), 1)
    in_group = ((rq * 43) >> 8 == qq).astype(F32)
    used = (jnp.dot(member, in_group, preferred_element_type=F32) > 0.5).astype(F32)
    lower = (((gi * 43) >> 8 == (ri * 43) >> 8) & (ri < gi)).astype(F32)
    rank = jnp.dot(lower, used, preferred_element_type=F32)
    code = jnp.where(used > 0.5, rank, -1.0)
    mine = jnp.sum(jnp.where(qq == f, rank, 0.0), axis=1, keepdims=True)
    delta = ((rq * 43) >> 8) - f
    base = jnp.zeros((NB, 128), F32)
    for d, slot, _ in OFFSETS:
        hit = (delta == -d) if d != 8 else ((delta == 8) | (delta == -8))
        base = jnp.where(hit, float(NBLK + slot), base)
    place = jnp.where(delta == 0, (rq - NBLK * f).astype(F32), base + mine)
    planv[...] = jnp.where(qq == 127, place, code).astype(jnp.int32)
    plan_cp = pltpu.make_async_copy(planv, plans, plan_sem)
    plan_cp.start()

    freq = consts[0:1, :]
    sign = consts[1:2, :]
    timed = consts[2:3, :] > 0.5
    inner = lax.broadcasted_iota(jnp.int32, (BLOCK, 128), 0)

    def table(b, carry):
        g = f * NBLK + b
        fr = mbf[g]

        def tally(i, n):
            return n + (mbf[i] < fr).astype(jnp.int32)

        first = lax.fori_loop(0, NB, tally, jnp.int32(0))
        pos = ((g - first) * BLOCK + inner).astype(F32)
        frame_pos = jnp.zeros((BLOCK, 128), F32) + fr.astype(F32)
        angle = jnp.where(jnp.broadcast_to(timed, (BLOCK, 128)), frame_pos, pos) * freq
        sn, cs = sin_cos(angle)
        cosv[rows(b), :] = cs
        sinv[rows(b), :] = sn * sign
        return carry

    lax.fori_loop(0, NBLK, table, 0)

    upv[...] = jnp.zeros_like(upv)
    for s in range(3):
        upv[s, s * RANK : (s + 1) * RANK, :] = up[s]

    weights_step(0)
    ld_tok.wait()
    ld_w.wait()
    ld_dn.wait()
    plan_cp.wait()

    lane = lax.broadcasted_iota(jnp.int32, (BLOCK, 128), 1)

    def rope(u, cs, sn):
        rot = jnp.where(
            lane < TIME_PAIRS,
            pltpu.roll(u, 128 - TIME_PAIRS, 1),
            jnp.where(
                lane < 2 * TIME_PAIRS,
                pltpu.roll(u, TIME_PAIRS, 1),
                jnp.where(
                    lane < 2 * TIME_PAIRS + SPACE_PAIRS,
                    pltpu.roll(u, 128 - SPACE_PAIRS, 1),
                    pltpu.roll(u, SPACE_PAIRS, 1),
                ),
            ),
        )
        return u * cs + rot * sn

    KC = 1280

    def compute(r):
        def step(k, carry):
            ks = pl.ds(pl.multiple_of(k * KC, 128), KC)
            xk = xg[rows(r), ks]
            keep = (k > 0).astype(F32)
            for s in range(3):
                part = jnp.dot(xk, wv[s, ks, :], preferred_element_type=F32)
                acc[s] = jnp.where(k > 0, acc[s], 0.0) + part
            low = lax.dot_general(xk, dnv[:, ks], (((1,), (1,)), ((), ())), preferred_element_type=F32)
            accl[...] = jnp.where(k > 0, accl[...], 0.0) + low
            return carry

        lax.fori_loop(0, MODEL_WIDTH // KC, step, 0)
        low = accl[...].astype(BF16)
        cs = cosv[rows(r), :]
        sn = sinv[rows(r), :]
        for s in range(3):
            y = acc[s] + jnp.dot(low, upv[s], preferred_element_type=F32)
            for a in range(HEADS):
                u = y[:, a * 128 : (a + 1) * 128]
                if s == 0:
                    qv[a, rows(r), :] = rope(u, cs, sn).astype(BF16)
                elif s == 1:
                    k = rope(u, cs, sn).astype(BF16)
                    own[a, r, 0] = k
                    pools[a][r, 0] = k
                else:
                    v = u.astype(BF16)
                    own[a, r, 1] = v
                    pools[a][r, 1] = v

    def kv_copy(a, slot, dst):
        return pltpu.make_async_remote_copy(
            src_ref=sb.at[a, slot], dst_ref=pools[a].at[NBLK + slot],
            send_sem=kv_send.at[a, slot], recv_sem=kv_recv.at[a, slot],
            device_id=(dst, h), device_id_type=MESH,
        )

    def send_slots(slots):
        picks = []
        for d, slot, rank_of in slots:
            dst, ok = target(d)
            col = dst if ok is None else jnp.clip(dst, 0, GROUPS - 1)
            idx = jnp.int32(0)
            for b in range(1, NBLK):
                idx = jnp.where(plans[f * NBLK + b, col] == rank_of, b, idx)
            picks.append((dst, ok, slot, idx))
        for a in range(HEADS):
            for dst, ok, slot, idx in picks:

                def go(dst=dst, slot=slot, idx=idx, a=a):
                    sb[a, slot] = own[a, idx]
                    kv_copy(a, slot, dst).start()

                if ok is None:
                    go()
                else:
                    pl.when(ok)(go)

    def finish(r):
        relay_up(r).wait_recv()
        share_far0(r).start()
        relay_dn(r).wait_recv()
        share_far1(r).start()
        own_other(r).wait_recv()
        share_dn(r).wait_recv()
        share_up(r).wait_recv()
        share_far0(r).wait_recv()
        share_far1(r).wait_recv()
        compute(r)
        for ready in range(NBLK):
            slots = [
                (d, first + i, i)
                for d, first, n in OFFSETS
                for i in range(n)
                if NBLK - n + i == ready
            ]
            if slots:

                @pl.when(r == ready)
                def _():
                    send_slots(slots)

    def ring(r, carry):
        own_up(r).wait_recv()
        relay_up(r).start()
        share_dn(r).start()
        own_dn(r).wait_recv()
        relay_dn(r).start()
        share_up(r).start()

        @pl.when(r + 2 < NBLK)
        def _():
            start_own(r + 2)

        for i, at in ((1, 0), (2, 1), (3, 3)):

            @pl.when(r == at)
            def _():
                weights_step(i)

        @pl.when(r > 0)
        def _():
            finish(r - 1)

        return carry

    lax.fori_loop(0, NBLK, ring, 0)
    od_ring = column_ring(
        lambda hh, half: odg.at[:, slice(0, RANK) if half is None else slice(32 * half, 32 * half + 32), lanes(hh)],
        3 * HEADS, odl,
    )
    for cp in ld_od:
        cp.wait()
    for a in range(HEADS):
        odg[a, :, lanes(h)] = odl[a]
    for i in range(3):
        od_ring[i].start()
    finish(NBLK - 1)
    advance(od_ring)
    spread(od_ring)
    settle(od_ring)

    def drain(r, carry):
        for cp in (own_up, own_dn, own_other, relay_up, relay_dn, share_dn, share_up, share_far0, share_far1):
            cp(r).wait_send()
        return carry

    scale = math.log2(math.e) / math.sqrt(HEAD_SIZE)

    def attend(a, b, carry):
        pool = pools[a]
        q = qv[a, rows(b), :]
        idx = [
            jnp.clip(plans[tabs[k, f * NBLK + b], 127], 0, NBLK + SLOTS - 1) for k in range(LISTED)
        ]
        top = None
        for k in range(0, LISTED, 2):
            kk = jnp.concatenate([pool[idx[k], 0], pool[idx[k + 1], 0]], axis=0)
            s = lax.dot_general(q, kk, (((1,), (1,)), ((), ())), preferred_element_type=F32)
            sc[:, k * 128 : (k + 2) * 128] = s
            part = jnp.maximum(s[:, :128], s[:, 128:])
            top = part if top is None else jnp.maximum(top, part)
        m = jnp.max(top, axis=1, keepdims=True)
        total = None
        o = None
        for k in range(0, LISTED, 2):
            p = jnp.exp2((sc[:, k * 128 : (k + 2) * 128] - m) * scale)
            t = p[:, :128] + p[:, 128:]
            total = t if total is None else total + t
            vv = jnp.concatenate([pool[idx[k], 1], pool[idx[k + 1], 1]], axis=0)
            po = jnp.dot(p.astype(BF16), vv, preferred_element_type=F32)
            o = po if o is None else o + po
        l = jnp.sum(total, axis=1, keepdims=True)
        attg[a, rows(b), lanes(h)] = (o / l).astype(BF16)
        return carry

    PARTS = 3
    PART = NBLK // PARTS * BLOCK
    STEPS = NBLK // PARTS

    def at_ring(i):
        a, c = i // PARTS, i % PARTS

        def view(hh, half):
            start = c * PART + (0 if half is None else half * (PART // 2))
            return attg.at[a, start : start + (PART if half is None else PART // 2), lanes(hh)]

        return column_ring(view, i)

    def project(i):
        a, c = i // PARTS, i % PARTS

        def go(b, carry):
            xa = attg[a, rows(b), :]
            part = jnp.dot(xa, wov[a].reshape(N_HEAD * 128, SHARD), preferred_element_type=F32)
            low = lax.dot_general(xa, odg[a], (((1,), (1,)), ((), ())), preferred_element_type=F32)
            if a == 0:
                oacc[rows(b), :] = part
                lacc[rows(b), :] = low
            elif a == 1:
                oacc[rows(b), :] += part
                lacc[rows(b), :] += low
            else:
                low = (lacc[rows(b), :] + low).astype(BF16)
                total = oacc[rows(b), :] + part
                out[rows(b), :] = (
                    total + jnp.dot(low, ou[...], preferred_element_type=F32)
                ).astype(BF16)
            return carry

        lax.fori_loop(c * STEPS, (c + 1) * STEPS, go, 0)

    ld_wo = pltpu.make_async_copy(wog, wov, loc_sem.at[6])
    rings = [at_ring(i) for i in range(PARTS * HEADS)]
    for i in range(PARTS * HEADS):
        a, c = i // PARTS, i % PARTS
        if c == 0:
            for d, first, n in OFFSETS:
                src = f8 if d == 8 else f - d

                def arrive(first=first, n=n, a=a):
                    for j in range(n):
                        kv_copy(a, first + j, f8).wait_recv()

                if d == 8:
                    arrive()
                else:
                    pl.when((src >= 0) & (src < GROUPS))(arrive)
        lax.fori_loop(c * STEPS, (c + 1) * STEPS, functools.partial(attend, a), 0)
        for j in range(3):
            rings[i][j].start()
        if i == 0:
            weights_step(4)
            ld_wo.start()
        if i >= 1:
            advance(rings[i - 1])
        if i >= 2:
            spread(rings[i - 2])
        if i == 3:
            ld_wo.wait()
        if i >= 3:
            settle(rings[i - 3])
            project(i - 3)
    advance(rings[8])
    spread(rings[7])
    settle(rings[6])
    project(6)
    spread(rings[8])
    settle(rings[7])
    project(7)
    settle(rings[8])
    project(8)

    for ring in rings + [od_ring]:
        for cp in ring:
            cp.wait_send()
    for j in range(1, N_HEAD):
        wz_copy(j).wait_send()
    for half in range(2):
        for stage in range(2):
            for kind in range(4):
                ring_copy(half, stage, kind).wait_send()
    lax.fori_loop(0, NBLK, drain, 0)
    for a in range(HEADS):
        for d, first, n in OFFSETS:
            dst, ok = target(d)

            def sent(first=first, n=n, a=a, dst=dst):
                for i in range(n):
                    kv_copy(a, first + i, f8).wait_send()

            if ok is None:
                sent()
            else:
                pl.when(ok)(sent)


def body(
    tokens,
    mask_block_frame,
    attended_key_blocks,
    frozen_query_key_value,
    query_key_value_down_weight,
    query_key_value_up_weight,
    frozen_output_weight,
    output_down_weight,
    output_up_weight,
):
    rows = tokens.shape[0]
    width = frozen_output_weight.shape[0]
    table = attended_key_blocks.T
    any_spec = pl.BlockSpec(memory_space=pl.ANY)
    vmem = pl.BlockSpec(memory_space=pltpu.VMEM)
    smem = pl.BlockSpec(memory_space=pltpu.SMEM)
    out, _ = pl.pallas_call(
        kernel,
        out_shape=(
            jax.ShapeDtypeStruct((rows, SHARD), BF16),
            jax.ShapeDtypeStruct((HEADS, N_HEAD, 128, SHARD), BF16),
        ),
        in_specs=[
            any_spec, vmem, smem, smem, vmem, any_spec, any_spec, vmem, any_spec, any_spec, vmem
        ],
        out_specs=(vmem, any_spec),
        scratch_shapes=[
            pltpu.VMEM((rows, MODEL_WIDTH), BF16),
            pltpu.VMEM((3, MODEL_WIDTH, width), BF16),
            pltpu.VMEM((3 * RANK, MODEL_WIDTH), BF16),
            pltpu.VMEM((3, 3 * RANK, width), BF16),
            pltpu.VMEM((rows, 128), F32),
            pltpu.VMEM((rows, 128), F32),
            pltpu.VMEM((NB, 128), jnp.int32),
            pltpu.SMEM((NB, 128), jnp.int32),
            pltpu.VMEM((3, BLOCK, width), F32),
            pltpu.VMEM((BLOCK, 3 * RANK), F32),
            pltpu.VMEM((HEADS, rows, 128), BF16),
            pltpu.VMEM((HEADS, NBLK, 2, BLOCK, 128), BF16),
            pltpu.VMEM((HEADS, SLOTS, 2, BLOCK, 128), BF16),
            pltpu.VMEM((NBLK + SLOTS, 2, BLOCK, 128), BF16),
            pltpu.VMEM((NBLK + SLOTS, 2, BLOCK, 128), BF16),
            pltpu.VMEM((NBLK + SLOTS, 2, BLOCK, 128), BF16),
            pltpu.VMEM((BLOCK, LISTED * BLOCK), F32),
            pltpu.VMEM((HEADS, N_HEAD, 128, SHARD), BF16),
            pltpu.VMEM((HEADS, RANK, 128), BF16),
            pltpu.VMEM((HEADS, RANK, N_HEAD * 128), BF16),
            pltpu.VMEM((HEADS, rows, N_HEAD * 128), BF16),
            pltpu.VMEM((rows, SHARD), F32),
            pltpu.VMEM((rows, RANK), F32),
            pltpu.SemaphoreType.DMA((7,)),
            pltpu.SemaphoreType.DMA((9, NBLK)),
            pltpu.SemaphoreType.DMA((9, NBLK)),
            pltpu.SemaphoreType.DMA((HEADS, SLOTS)),
            pltpu.SemaphoreType.DMA((HEADS, SLOTS)),
            pltpu.SemaphoreType.DMA,
            pltpu.SemaphoreType.DMA((N_HEAD,)),
            pltpu.SemaphoreType.DMA((N_HEAD,)),
            pltpu.SemaphoreType.DMA((4, 4)),
            pltpu.SemaphoreType.DMA((4, 4)),
            pltpu.SemaphoreType.DMA((9, 3 * HEADS + 1)),
            pltpu.SemaphoreType.DMA((9, 3 * HEADS + 1)),
        ],
        compiler_params=pltpu.CompilerParams(
            collective_id=0, has_side_effects=True, vmem_limit_bytes=62 * 1024 * 1024
        ),
    )(
        tokens,
        table,
        table,
        mask_block_frame,
        jnp.asarray(rope_constants()),
        frozen_query_key_value.transpose(1, 0, 2),
        query_key_value_down_weight.T,
        query_key_value_up_weight.transpose(1, 0, 2),
        frozen_output_weight.reshape(HEADS, 128, MODEL_WIDTH),
        output_down_weight.T,
        output_up_weight,
    )
    return out


def solution(mesh):
    return jax.shard_map(
        body,
        mesh=mesh,
        in_specs=(
            P("frame", "head"),
            P(),
            P(),
            P(None, None, "head"),
            P(),
            P(None, None, "head"),
            P("head", None),
            P("head", None),
            P(None, "head"),
        ),
        out_specs=P("frame", "head"),
        check_vma=False,
    )
```
